32 devices in a mesh: member: 2 (over x), tile: 16 (over z, y, core).
Axes of the slice: x: 2, y: 2, z: 4, core: 2. Of those that a mesh axis runs over, the one named last changes fastest.
Arguments:
- noise_seeds: int32 [4], P('member'), parts along dimension 0, may hold values from 0 to 2147483646
- diffusivity: float32 [128, 256], P('tile'), may hold values from 0.03 to 0.24
- wet_mask: int32 [128, 256], P('tile'), may hold values 0 or 1
- vert_factor: float32 [75, 75], replicated, may hold values from -0.75 to 0.75
- norm_scale: float32 [128, 256], P('tile'), may hold values from 0.5 to 8
- obs_cell: int32 [16, 16, 128], P('tile'), may hold values from 0 to 2046, as said below
- obs_frac: float32 [16, 16, 2, 128], P('tile'), may hold values from 0 to 1
- obs_count: int32 [16, 16], P('tile'), may hold values from 32 to 128, as said below
Outputs:
- perturbation: bfloat16 [150, 128, 256], P('member', 'tile'), parts along dimension 0
- profiles: bfloat16 [16, 16, 150, 128], P('tile', None, 'member'), parts along dimension 2
The draws below stay inside these ranges and needn't reach their ends.
There are 2 independent parts, one for each index of `member`. The reference program is written for one: setup_inputs(seed, part) draws one part's arguments, and reference() takes and returns one part's arrays. A program takes and returns all parts, laid end to end along the dimension named above; an argument that names none is the same for every part. Nothing has to cross between parts.
Inputs may be any that keep to these rules, and one draw needn't show every extreme that they name: `obs_cell`: each entry is row * 256 + column of an anchor cell in the owner tile's block of 8 x 256 cells, with column below 255, and row below 7 where the owner is the last tile. `obs_count`: some owner receives 128 live slots from every holder, and other counts vary by owner.
All inputs are finite; a program needn't handle non-finite values. No bound on the sum of `wet_mask` on one device may be relied on, other than what follows from the above.
Results may differ from the reference program's by a relative error of at most 0.0045.
Values may be sent and summed in bfloat16 or wider, within the bound.
No kernel may reach another device: no remote copies, remote signals or barrier semaphores. Data moves between devices by JAX's collectives and lax.ppermute only.
A program may use at most 64 MiB of HBM per device.

```python
import math
import jax
import jax.numpy as jnp
from jax import lax

L = 75
STEPS = 8
RY = 8
NX = 256
CAP = 128
NY = 128
N_TILE = 16


def draw_obs_cell(key, part):
    owner = jnp.arange(N_TILE, dtype=jnp.int32)[None, :, None]
    row_top = jnp.where(owner == N_TILE - 1, RY - 1, RY).astype(jnp.int32)
    row_top = jnp.broadcast_to(row_top, (N_TILE, N_TILE, CAP))
    rows_drawn = jax.random.randint(jax.random.fold_in(key, 11), (N_TILE, N_TILE, CAP), 0, row_top, dtype=jnp.int32)
    cols_drawn = jax.random.randint(jax.random.fold_in(key, 12), (N_TILE, N_TILE, CAP), 0, NX - 1, dtype=jnp.int32)
    return rows_drawn * NX + cols_drawn


def draw_obs_count(key, part):
    base_counts = jax.random.randint(jax.random.fold_in(key, 21), (N_TILE, N_TILE), CAP // 4, CAP // 2 + 1, dtype=jnp.int32)
    busy_counts = jax.random.randint(jax.random.fold_in(key, 22), (N_TILE, N_TILE), CAP // 2, CAP + 1, dtype=jnp.int32)
    hot_owners = jax.random.randint(jax.random.fold_in(key, 23), (3,), 0, N_TILE, dtype=jnp.int32)
    owner_ids = jnp.arange(N_TILE, dtype=jnp.int32)
    is_hot = jnp.any(owner_ids[None, :] == hot_owners[:, None], axis=0)
    counts = jnp.where(is_hot[None, :], busy_counts, base_counts)
    counts = jnp.where(owner_ids[None, :] == hot_owners[0], CAP, counts)
    corner = jax.random.randint(jax.random.fold_in(key, 24), (2,), 0, N_TILE, dtype=jnp.int32)
    counts = counts.at[corner[0], corner[1]].set(CAP)
    return counts.astype(jnp.int32)


def with_ends(values, stream_key, least, high):
    longest = values.shape.index(max(values.shape))
    spots = []
    for shift in (0, 1):
        where = [jax.random.randint(jax.random.fold_in(stream_key, axis), (), 0, length) for axis, length in enumerate(values.shape)]
        where[longest] = (where[longest] + shift) % values.shape[longest]
        spots.append(tuple(where))
    return values.at[spots[0]].set(least).at[spots[1]].set(high)


def block_scale(stream_key, extent, shards, smallest, high):
    level, own = 1.0, jax.random.fold_in(stream_key, 6)
    for dim, blocks in shards:
        heights = jnp.exp(jax.random.uniform(jax.random.fold_in(own, dim), (blocks,), jnp.float32, smallest / len(shards), high / len(shards)))
        level = level * jnp.repeat(heights, extent[dim] // blocks).reshape([-1 if axis == dim else 1 for axis in range(len(extent))])
    return level


def scatter_about(stream_key, shape, scale, bound, kind=jnp.bfloat16):
    return jnp.clip(scale * jax.random.normal(stream_key, shape, jnp.float32), -bound, bound).astype(kind)


def setup_inputs(seed: int = 0, part: int = 0) -> dict:
    key_of = jax.random.split(jax.random.key(seed), 9)
    part_splits = jax.random.split(jax.random.fold_in(key_of[8], part), 9)
    noise_seeds = jax.random.randint(part_splits[0], (2,), 0, 2147483647).astype(jnp.int32)
    diffusivity = jnp.clip(jnp.exp(math.log(0.24) - 2.0794415 * jax.random.uniform(key_of[1], (NY, NX), jnp.float32) ** block_scale(key_of[1], (NY, NX), ((0, 16),), -0.2, 0.2)), 0.03, 0.24)
    wet_mask = with_ends((jax.random.randint(key_of[2], (NY, NX), 0, 10) < 7).astype(jnp.int32), jax.random.fold_in(key_of[2], 1), 0, 1)
    vert_factor = scatter_about(key_of[3], (L, L), L ** -0.5, 0.75, jnp.float32)
    norm_scale = jnp.clip(jnp.exp(math.log(8.0) - 2.7725887 * jax.random.uniform(key_of[4], (NY, NX), jnp.float32) ** block_scale(key_of[4], (NY, NX), ((0, 16),), -0.2, 0.2)), 0.5, 8.0)
    obs_cell = draw_obs_cell(jax.random.fold_in(key_of[8], 71), part)
    obs_frac = jnp.clip(1.0 * jax.random.uniform(key_of[6], (N_TILE, N_TILE, 2, CAP), jnp.float32) ** block_scale(key_of[6], (N_TILE, N_TILE, 2, CAP), ((0, 16),), -0.2, 0.2), 0.0, 1.0)
    obs_count = draw_obs_count(jax.random.fold_in(key_of[8], 71), part)
    return {"noise_seeds": noise_seeds, "diffusivity": diffusivity, "wet_mask": wet_mask, "vert_factor": vert_factor, "norm_scale": norm_scale, "obs_cell": obs_cell, "obs_frac": obs_frac, "obs_count": obs_count}


def scramble(hashed):
    hashed = jnp.bitwise_xor(hashed, hashed >> 16 & 65535) * -2048144789
    hashed = jnp.bitwise_xor(hashed, hashed >> 13 & 524287) * -1028477387
    return jnp.bitwise_xor(hashed, hashed >> 16 & 65535)

def cell_noise(noise_seeds, counter):
    hashed = scramble(counter * -1640531535 + noise_seeds[0])
    hashed = scramble(jnp.bitwise_xor(hashed, noise_seeds[1]))
    uniform = ((hashed >> 8 & 16777215).astype(jnp.float32) + 0.5) * (1.0 / 16777216.0)
    return (uniform - 0.5) * 3.4641016151377544

def face_terms(wet_pad):
    face_rows = jnp.sqrt(wet_pad[1:] * wet_pad[:-1])
    face_cols = jnp.sqrt(wet_pad[:, 1:] * wet_pad[:, :-1])
    return (face_rows, face_cols)

def diffuse(padded, face_rows, face_cols):
    flux_rows = face_rows[None] * (padded[:, 1:] - padded[:, :-1])
    flux_cols = face_cols[None] * (padded[:, :, 1:] - padded[:, :, :-1])
    zero_col = jnp.zeros(flux_cols.shape[:2] + (1,), jnp.float32)
    net_cols = jnp.concatenate([flux_cols, zero_col], 2) - jnp.concatenate([zero_col, flux_cols], 2)
    return padded[:, 1:-1] + (flux_rows[:, 1:] - flux_rows[:, :-1]) + net_cols[:, 1:-1]

def bilinear(flat_field, anchor, frac_y, frac_x, columns):
    corner_nw = jnp.take(flat_field, anchor, axis=1).astype(jnp.float32)
    corner_ne = jnp.take(flat_field, anchor + 1, axis=1).astype(jnp.float32)
    corner_sw = jnp.take(flat_field, anchor + columns, axis=1).astype(jnp.float32)
    corner_se = jnp.take(flat_field, anchor + columns + 1, axis=1).astype(jnp.float32)
    blended = (1.0 - frac_y) * ((1.0 - frac_x) * corner_nw + frac_x * corner_ne) + frac_y * ((1.0 - frac_x) * corner_sw + frac_x * corner_se)
    return blended

def reference(noise_seeds, diffusivity, wet_mask, vert_factor, norm_scale, obs_cell, obs_frac, obs_count):
    wet_float = wet_mask.astype(jnp.float32)
    wet_kappa = diffusivity * wet_float
    wet_pad = jnp.pad(wet_kappa, ((1, 1), (0, 0)))
    face_rows, face_cols = face_terms(wet_pad)
    level_ids = lax.broadcasted_iota(jnp.int32, (L, NY, NX), 0)
    row_ids = lax.broadcasted_iota(jnp.int32, (L, NY, NX), 1)
    col_ids = lax.broadcasted_iota(jnp.int32, (L, NY, NX), 2)
    counter = (level_ids * NY + row_ids) * NX + col_ids
    state_field = cell_noise(noise_seeds, counter) * wet_float[None]
    for outer_step in range(STEPS):
        padded = jnp.pad(state_field, ((0, 0), (1, 1), (0, 0)))
        state_field = diffuse(padded, face_rows, face_cols)
    mixed_levels = jnp.dot(vert_factor, state_field.reshape(L, NY * NX), precision=lax.Precision.HIGHEST, preferred_element_type=jnp.float32)
    perturbation = (mixed_levels.reshape(L, NY, NX) * norm_scale[None]).astype(jnp.bfloat16)
    flat_field = jnp.concatenate([perturbation, jnp.zeros((L, 1, NX), jnp.bfloat16)], 1).reshape(L, (NY + 1) * NX)
    owner_base = (jnp.arange(N_TILE, dtype=jnp.int32) * (RY * NX)).astype(jnp.int32)
    slot_ids = jnp.arange(CAP, dtype=jnp.int32)

    def one_holder(inputs):
        cells, fracs, counts = inputs
        anchor = (cells + owner_base[:, None]).astype(jnp.int32)
        blended = bilinear(flat_field, anchor, fracs[:, 0], fracs[:, 1], NX)
        profile = jnp.transpose(blended, (1, 0, 2)).astype(jnp.bfloat16)
        live_slot = slot_ids[None, None, :] < counts[:, None, None]
        return jnp.where(live_slot, profile, jnp.zeros_like(profile))
    profiles = lax.map(one_holder, (obs_cell, obs_frac, obs_count))
    return (perturbation, profiles)
```

```python
import jax
import jax.numpy as jnp
from jax import lax
from jax.experimental import pallas as pl
from jax.experimental.pallas import tpu as pltpu
from jax.sharding import PartitionSpec as P

STEPS = 8
LANES = 128
SUB = 8
EXACT = lax.Precision.HIGHEST
F32 = jnp.float32
I32 = jnp.int32
GOLDEN = -1640531535
ROOT12 = 3.4641016151377544
VMEM = pl.BlockSpec(memory_space=pltpu.VMEM)
SMEM = pl.BlockSpec(memory_space=pltpu.SMEM)


def up(value, unit):
    return -(-value // unit) * unit


def wrapped(value):
    return (value + 2**31) % 2**32 - 2**31


def iota(shape, axis):
    return lax.broadcasted_iota(I32, shape, axis)


def split_columns(columns):
    half = columns // 2
    col = iota((columns, columns), 0)
    place = iota((columns, columns), 1)
    source = jnp.where(place < half, 2 * place, 2 * (place - half) + 1)
    return col == source


def pack_kernel(diff_ref, wet_ref, norm_ref, cell_ref, frac_ref, count_ref, out_ref, norm_out):
    tile_rows, columns = diff_ref.shape
    half = columns // 2
    owners = cell_ref.shape[0]
    kappa = diff_ref[...] * wet_ref[...].astype(F32)
    both = jnp.concatenate([kappa, norm_ref[...]], 0)
    parted = jnp.dot(
        both, split_columns(columns).astype(F32), precision=EXACT, preferred_element_type=F32
    )
    kappa_even, kappa_odd = parted[:tile_rows, :half], parted[:tile_rows, half:]
    norm_even, norm_odd = parted[tile_rows:, :half], parted[tile_rows:, half:]
    norm_out[:tile_rows] = norm_even
    norm_out[tile_rows:] = norm_odd
    cell = cell_ref[...]
    row = jnp.zeros_like(cell)
    for step in range(1, tile_rows):
        row = row + (cell >= step * columns).astype(I32)
    col = cell - row * columns
    pos_y = row.astype(F32) + frac_ref[:, 0, :]
    pos_x = col.astype(F32) + frac_ref[:, 1, :]
    lane = iota((1, LANES), 1)
    for owner in range(owners):
        out_ref[owner, :tile_rows, :] = kappa_even
        out_ref[owner, tile_rows : 2 * tile_rows, :] = kappa_odd
        live = lane < count_ref[0, owner]
        tail = jnp.concatenate(
            [
                norm_even[:1],
                norm_odd[:1],
                pos_x[owner : owner + 1],
                jnp.where(live, pos_y[owner : owner + 1], -2.0),
                jnp.zeros((SUB - 4, LANES), F32),
            ],
            0,
        )
        out_ref[owner, 2 * tile_rows :, :] = tail


def mix(hashed, second):
    hashed = (hashed ^ lax.shift_right_logical(hashed, 16)) * -2048144789
    hashed = (hashed ^ lax.shift_right_logical(hashed, 13)) * -1028477387
    hashed = hashed ^ lax.shift_right_logical(hashed, 16)
    return hashed


def noise_kernel(total_rows, tile_rows, columns, seed_ref, out_ref):
    planes, levels, _ = out_ref.shape
    first_row = lax.axis_index("tile") * tile_rows - STEPS
    step_level = wrapped(total_rows * columns * GOLDEN)
    shape = (SUB, LANES)
    base = iota(shape, 0) * step_level + iota(shape, 1) * wrapped(2 * GOLDEN)
    gain = ROOT12 / 16777216.0
    shift = (0.5 / 16777216.0 - 0.5) * ROOT12
    origin = first_row * wrapped(columns * GOLDEN) + seed_ref[0]
    second = seed_ref[1]

    def one_tile(block, carry):
        start = origin + block * wrapped(SUB * step_level)
        for plane in range(planes):
            offset = start + wrapped(((plane // 2) * columns + plane % 2) * GOLDEN)
            hashed = mix(mix(base + offset, None) ^ second, None)
            level = pl.multiple_of(block * SUB, SUB)
            drawn = lax.shift_right_logical(hashed, 8).astype(F32)
            out_ref[plane, pl.ds(level, SUB), :] = drawn * gain + shift
        return carry

    lax.fori_loop(0, levels // SUB, one_tile, 0)


def field_kernel(
    tiles, noise_ref, recv_ref, norm_ref, vert_ref, prof_ref, field_ref,
    even_ref, odd_ref, root_ref, keep_ref, gain_ref, vert_pad, state_ref,
):
    planes, levels, half = noise_ref.shape
    rows = planes // 2
    columns = 2 * half
    tile_rows = norm_ref.shape[0] // 2
    depth = vert_ref.shape[0]
    out_rows = tile_rows + 1
    tile = lax.axis_index("tile")

    even_ref[...] = jnp.zeros_like(even_ref)
    odd_ref[...] = jnp.zeros_like(odd_ref)
    for place, (shift, count) in enumerate(((-1, tile_rows), (0, tile_rows), (1, tile_rows), (2, 1))):
        source = tile + shift
        valid = ((source >= 0) & (source < tiles)).astype(F32)
        source = jnp.clip(source, 0, tiles - 1)
        start = place * tile_rows
        even_ref[start : start + count] = recv_ref[source, :count, :] * valid
        odd_ref[start : start + count] = recv_ref[source, tile_rows : tile_rows + count, :] * valid
    kappa_even, kappa_odd = even_ref[...], odd_ref[...]
    below = jnp.clip(tile + 1, 0, tiles - 1)
    even_ref[...] = jnp.sqrt(kappa_even)
    odd_ref[...] = jnp.sqrt(kappa_odd)
    root_even, root_odd = even_ref[...], odd_ref[...]
    lane = iota((1, LANES), 1)
    first, last = lane == 0, lane == LANES - 1
    inner = slice(1, rows - 1)
    for parity, (mine, other, mine_ref, edge, turn) in enumerate((
        (root_even, root_odd, even_ref, first, 1),
        (root_odd, root_even, odd_ref, last, LANES - 1),
    )):
        turned = jnp.where(edge, 0.0, pltpu.roll(other, turn, 1))
        near = mine_ref[: rows - 2] + mine_ref[2:rows] + (other + turned)[inner]
        keep = 1.0 - mine[inner] * near
        gain = mine[inner] * mine[inner]
        for row in range(rows):
            spread = (SUB, LANES)
            root_ref[2 * row + parity] = jnp.broadcast_to(mine[row : row + 1], spread)
            if 0 < row < rows - 1:
                keep_ref[2 * row + parity] = jnp.broadcast_to(keep[row - 1 : row], spread)
                gain_ref[2 * row + parity] = jnp.broadcast_to(gain[row - 1 : row], spread)
    own = slice(STEPS, STEPS + out_rows)
    scales = []
    for parity, (root, kappa) in enumerate(((root_even, kappa_even), (root_odd, kappa_odd))):
        wet = kappa[own] > 0.0
        inverse = jnp.where(wet, root[own] / jnp.where(wet, kappa[own], 1.0), 0.0)
        norm = jnp.concatenate(
            [
                norm_ref[parity * tile_rows : (parity + 1) * tile_rows],
                recv_ref[below, 2 * tile_rows + parity : 2 * tile_rows + parity + 1, :],
            ],
            0,
        )
        scales.append(inverse * norm)

    block = (SUB, LANES)
    first8, last8 = iota(block, 1) == 0, iota(block, 1) == LANES - 1

    def diffuse(part, carry):
        span = pl.ds(pl.multiple_of(part * SUB, SUB), SUB)
        even = [noise_ref[2 * row, span, :] * root_ref[2 * row] for row in range(rows)]
        odd = [noise_ref[2 * row + 1, span, :] * root_ref[2 * row + 1] for row in range(rows)]
        for step in range(STEPS):
            next_even, next_odd = [], []
            for j in range(1, len(even) - 1):
                at = 2 * (j + step)
                e, o = even[j], odd[j]
                west = jnp.where(first8, 0.0, pltpu.roll(o, 1, 1))
                east = jnp.where(last8, 0.0, pltpu.roll(e, LANES - 1, 1))
                sum_e = (even[j - 1] + even[j + 1]) + (o + west)
                sum_o = (odd[j - 1] + odd[j + 1]) + (e + east)
                next_even.append(keep_ref[at] * e + gain_ref[at] * sum_e)
                next_odd.append(keep_ref[at + 1] * o + gain_ref[at + 1] * sum_o)
            even, odd = next_even, next_odd
        for row in range(out_rows):
            state_ref[span, row * columns : row * columns + half] = even[row]
            state_ref[span, row * columns + half : (row + 1) * columns] = odd[row]
        return carry

    lax.fori_loop(0, levels // SUB, diffuse, 0)

    vert_pad[...] = jnp.zeros_like(vert_pad)
    vert_pad[:depth, :depth] = vert_ref[...]
    factor = vert_pad[...]
    for row in range(out_rows):
        scale = jnp.concatenate([scales[0][row : row + 1], scales[1][row : row + 1]], 1)
        mixed = jnp.dot(
            factor,
            state_ref[:, row * columns : (row + 1) * columns],
            precision=EXACT,
            preferred_element_type=F32,
        )
        field_ref[row * levels : (row + 1) * levels, :] = (mixed * scale).astype(jnp.bfloat16)

    place = iota((columns, 2 * LANES), 0)
    col = jnp.where(place < half, 2 * place, 2 * (place - half) + 1).astype(F32)

    def interpolate(pair, carry):
        tails = [recv_ref[2 * pair + k, 2 * tile_rows :, :] for k in range(2)]
        pos_x = jnp.concatenate([tails[0][2:3], tails[1][2:3]], 1)
        pos_y = jnp.concatenate([tails[0][3:4], tails[1][3:4]], 1)
        hat = jnp.maximum(1.0 - jnp.abs(pos_x - col), 0.0).astype(jnp.bfloat16)
        total = None
        for row in range(out_rows):
            along = jnp.dot(
                field_ref[row * levels : (row + 1) * levels, :], hat, preferred_element_type=F32
            )
            weight = jnp.maximum(1.0 - jnp.abs(pos_y - float(row)), 0.0)
            total = along * weight if total is None else total + along * weight
        rounded = total[:depth].astype(jnp.bfloat16)
        prof_ref[2 * pair] = rounded[:, :LANES]
        prof_ref[2 * pair + 1] = rounded[:, LANES:]
        return carry

    lax.fori_loop(0, tiles // 2, interpolate, 0)


def weave_kernel(field_ref, out_ref, flat_ref):
    depth, tile_rows, columns = out_ref.shape
    levels = field_ref.shape[0] // (tile_rows + 1)
    half = columns // 2
    place = iota((columns, columns), 0)
    col = iota((columns, columns), 1)
    source = jnp.where(place < half, 2 * place, 2 * (place - half) + 1)
    weave = (col == source).astype(jnp.bfloat16)
    for row in range(tile_rows):
        woven = jnp.dot(
            field_ref[row * levels : (row + 1) * levels, :], weave, preferred_element_type=F32
        )
        flat_ref[:, row, :] = woven
    out_ref[...] = flat_ref[:depth].astype(jnp.bfloat16)


def body(
    noise_seeds, diffusivity, wet_mask, vert_factor, norm_scale, obs_cell, obs_frac, obs_count
):
    tile_rows, columns = diffusivity.shape
    depth = vert_factor.shape[0]
    levels = up(depth, 2 * SUB)
    tiles = lax.axis_size("tile")
    total_rows = tile_rows * tiles
    half = columns // 2
    rows = tile_rows + 1 + 2 * STEPS
    slots = obs_cell.shape[2]

    packed, norm_split = pl.pallas_call(
        pack_kernel,
        out_shape=(
            jax.ShapeDtypeStruct((tiles, 2 * tile_rows + SUB, LANES), F32),
            jax.ShapeDtypeStruct((2 * tile_rows, half), F32),
        ),
        in_specs=[VMEM] * 5 + [SMEM],
        out_specs=(VMEM, VMEM),
        name="pack",
    )(diffusivity, wet_mask, norm_scale, obs_cell[0], obs_frac[0], obs_count)
    received = lax.all_to_all(packed, "tile", split_axis=0, concat_axis=0, tiled=True)

    noise = pl.pallas_call(
        lambda *refs: noise_kernel(total_rows, tile_rows, columns, *refs),
        out_shape=jax.ShapeDtypeStruct((2 * rows, levels, half), F32),
        in_specs=[SMEM],
        out_specs=VMEM,
        name="noise",
    )(noise_seeds)

    flat = (2 * rows, SUB, LANES)
    answers, field = pl.pallas_call(
        lambda *refs: field_kernel(tiles, *refs),
        out_shape=(
            jax.ShapeDtypeStruct((tiles, depth, slots), jnp.bfloat16),
            jax.ShapeDtypeStruct(((tile_rows + 1) * levels, columns), jnp.bfloat16),
        ),
        in_specs=[VMEM] * 4,
        out_specs=(VMEM, VMEM),
        scratch_shapes=[
            pltpu.VMEM((up(rows, SUB), half), F32),
            pltpu.VMEM((up(rows, SUB), half), F32),
            pltpu.VMEM(flat, F32),
            pltpu.VMEM(flat, F32),
            pltpu.VMEM(flat, F32),
            pltpu.VMEM((levels, levels), F32),
            pltpu.VMEM((levels, (tile_rows + 1) * columns), F32),
        ],
        name="field",
    )(noise, received, norm_split, vert_factor)
    profiles = lax.all_to_all(answers, "tile", split_axis=0, concat_axis=0, tiled=True)

    perturbation = pl.pallas_call(
        weave_kernel,
        out_shape=jax.ShapeDtypeStruct((depth, tile_rows, columns), jnp.bfloat16),
        in_specs=[VMEM],
        out_specs=VMEM,
        scratch_shapes=[pltpu.VMEM((levels, tile_rows, columns), F32)],
        name="weave",
    )(field)
    return (perturbation, profiles[None])


def solution(mesh):
    in_specs = (
        P("member"),
        P("tile", None),
        P("tile", None),
        P(),
        P("tile", None),
        P("tile", None, None),
        P("tile", None, None, None),
        P("tile", None),
    )
    out_specs = (P("member", "tile", None), P("tile", None, "member", None))
    return jax.shard_map(body, mesh=mesh, in_specs=in_specs, out_specs=out_specs, check_vma=False)
```

```python
import jax
import jax.numpy as jnp
from jax import lax
from jax.experimental import pallas as pl
from jax.experimental.pallas import tpu as pltpu
from jax.sharding import PartitionSpec as P

STEPS = 8
LANES = 128
SUB = 8
EXACT = lax.Precision.HIGHEST
F32 = jnp.float32
I32 = jnp.int32
GOLDEN = -1640531535
ROOT12 = 3.4641016151377544
VMEM = pl.BlockSpec(memory_space=pltpu.VMEM)
SMEM = pl.BlockSpec(memory_space=pltpu.SMEM)
LIMIT = pltpu.CompilerParams(vmem_limit_bytes=24 << 20)


def resident(array):
    return pltpu.with_memory_space_constraint(array, pltpu.VMEM)


def up(value, unit):
    return -(-value // unit) * unit


def wrapped(value):
    return (value + 2**31) % 2**32 - 2**31


def iota(shape, axis):
    return lax.broadcasted_iota(I32, shape, axis)


def split_columns(columns):
    half = columns // 2
    col = iota((columns, columns), 0)
    place = iota((columns, columns), 1)
    source = jnp.where(place < half, 2 * place, 2 * (place - half) + 1)
    return col == source


def pack_kernel(diff_ref, wet_ref, norm_ref, cell_ref, frac_ref, count_ref, out_ref, norm_out):
    tile_rows, columns = diff_ref.shape
    half = columns // 2
    owners = cell_ref.shape[0]
    kappa = diff_ref[...] * wet_ref[...].astype(F32)
    both = jnp.concatenate([kappa, norm_ref[...]], 0)
    parted = jnp.dot(
        both, split_columns(columns).astype(F32), precision=EXACT, preferred_element_type=F32
    )
    kappa_even, kappa_odd = parted[:tile_rows, :half], parted[:tile_rows, half:]
    norm_even, norm_odd = parted[tile_rows:, :half], parted[tile_rows:, half:]
    norm_out[:tile_rows] = norm_even
    norm_out[tile_rows:] = norm_odd
    cell = cell_ref[...]
    row = jnp.zeros_like(cell)
    for step in range(1, tile_rows):
        row = row + (cell >= step * columns).astype(I32)
    col = cell - row * columns
    pos_y = row.astype(F32) + frac_ref[:, 0, :]
    pos_x = col.astype(F32) + frac_ref[:, 1, :]
    lane = iota((1, LANES), 1)
    for owner in range(owners):
        out_ref[owner, :tile_rows, :] = kappa_even
        out_ref[owner, tile_rows : 2 * tile_rows, :] = kappa_odd
        live = lane < count_ref[0, owner]
        tail = jnp.concatenate(
            [
                norm_even[:1],
                norm_odd[:1],
                pos_x[owner : owner + 1],
                jnp.where(live, pos_y[owner : owner + 1], -2.0),
                jnp.zeros((SUB - 4, LANES), F32),
            ],
            0,
        )
        out_ref[owner, 2 * tile_rows :, :] = tail


def mix(hashed, second):
    hashed = (hashed ^ lax.shift_right_logical(hashed, 16)) * -2048144789
    hashed = (hashed ^ lax.shift_right_logical(hashed, 13)) * -1028477387
    hashed = hashed ^ lax.shift_right_logical(hashed, 16)
    return hashed


def noise_kernel(total_rows, tile_rows, columns, seed_ref, out_ref):
    planes, levels, _ = out_ref.shape
    first_row = lax.axis_index("tile") * tile_rows - STEPS
    step_level = wrapped(total_rows * columns * GOLDEN)
    shape = (SUB, LANES)
    base = iota(shape, 0) * step_level + iota(shape, 1) * wrapped(2 * GOLDEN)
    gain = ROOT12 / 16777216.0
    shift = (0.5 / 16777216.0 - 0.5) * ROOT12
    origin = first_row * wrapped(columns * GOLDEN) + seed_ref[0]
    second = seed_ref[1]

    def one_tile(block, carry):
        start = origin + block * wrapped(SUB * step_level)
        for plane in range(planes):
            offset = start + wrapped(((plane // 2) * columns + plane % 2) * GOLDEN)
            hashed = mix(mix(base + offset, None) ^ second, None)
            level = pl.multiple_of(block * SUB, SUB)
            drawn = lax.shift_right_logical(hashed, 8).astype(F32)
            out_ref[plane, pl.ds(level, SUB), :] = drawn * gain + shift
        return carry

    lax.fori_loop(0, levels // SUB, one_tile, 0)


def field_kernel(
    tiles, noise_ref, recv_ref, norm_ref, vert_ref, prof_ref, field_ref,
    even_ref, odd_ref, root_ref, keep_ref, gain_ref, vert_pad, state_ref,
):
    planes, levels, half = noise_ref.shape
    rows = planes // 2
    columns = 2 * half
    tile_rows = norm_ref.shape[0] // 2
    depth = vert_ref.shape[0]
    out_rows = tile_rows + 1
    tile = lax.axis_index("tile")

    even_ref[...] = jnp.zeros_like(even_ref)
    odd_ref[...] = jnp.zeros_like(odd_ref)
    for place, (shift, count) in enumerate(((-1, tile_rows), (0, tile_rows), (1, tile_rows), (2, 1))):
        source = tile + shift
        valid = ((source >= 0) & (source < tiles)).astype(F32)
        source = jnp.clip(source, 0, tiles - 1)
        start = place * tile_rows
        even_ref[start : start + count] = recv_ref[source, :count, :] * valid
        odd_ref[start : start + count] = recv_ref[source, tile_rows : tile_rows + count, :] * valid
    kappa_even, kappa_odd = even_ref[...], odd_ref[...]
    below = jnp.clip(tile + 1, 0, tiles - 1)
    even_ref[...] = jnp.sqrt(kappa_even)
    odd_ref[...] = jnp.sqrt(kappa_odd)
    root_even, root_odd = even_ref[...], odd_ref[...]
    lane = iota((1, LANES), 1)
    first, last = lane == 0, lane == LANES - 1
    inner = slice(1, rows - 1)
    for parity, (mine, other, mine_ref, edge, turn) in enumerate((
        (root_even, root_odd, even_ref, first, 1),
        (root_odd, root_even, odd_ref, last, LANES - 1),
    )):
        turned = jnp.where(edge, 0.0, pltpu.roll(other, turn, 1))
        near = mine_ref[: rows - 2] + mine_ref[2:rows] + (other + turned)[inner]
        keep = 1.0 - mine[inner] * near
        gain = mine[inner] * mine[inner]
        for row in range(rows):
            spread = (SUB, LANES)
            root_ref[2 * row + parity] = jnp.broadcast_to(mine[row : row + 1], spread)
            if 0 < row < rows - 1:
                keep_ref[2 * row + parity] = jnp.broadcast_to(keep[row - 1 : row], spread)
                gain_ref[2 * row + parity] = jnp.broadcast_to(gain[row - 1 : row], spread)
    own = slice(STEPS, STEPS + out_rows)
    scales = []
    for parity, (root, kappa) in enumerate(((root_even, kappa_even), (root_odd, kappa_odd))):
        wet = kappa[own] > 0.0
        inverse = jnp.where(wet, root[own] / jnp.where(wet, kappa[own], 1.0), 0.0)
        norm = jnp.concatenate(
            [
                norm_ref[parity * tile_rows : (parity + 1) * tile_rows],
                recv_ref[below, 2 * tile_rows + parity : 2 * tile_rows + parity + 1, :],
            ],
            0,
        )
        scales.append(inverse * norm)

    block = (SUB, LANES)
    first8, last8 = iota(block, 1) == 0, iota(block, 1) == LANES - 1

    def diffuse(part, carry):
        span = pl.ds(pl.multiple_of(part * SUB, SUB), SUB)
        even = [noise_ref[2 * row, span, :] * root_ref[2 * row] for row in range(rows)]
        odd = [noise_ref[2 * row + 1, span, :] * root_ref[2 * row + 1] for row in range(rows)]
        for step in range(STEPS):
            next_even, next_odd = [], []
            for j in range(1, len(even) - 1):
                at = 2 * (j + step)
                e, o = even[j], odd[j]
                west = jnp.where(first8, 0.0, pltpu.roll(o, 1, 1))
                east = jnp.where(last8, 0.0, pltpu.roll(e, LANES - 1, 1))
                sum_e = (even[j - 1] + even[j + 1]) + (o + west)
                sum_o = (odd[j - 1] + odd[j + 1]) + (e + east)
                next_even.append(keep_ref[at] * e + gain_ref[at] * sum_e)
                next_odd.append(keep_ref[at + 1] * o + gain_ref[at + 1] * sum_o)
            even, odd = next_even, next_odd
        for row in range(out_rows):
            state_ref[span, row * columns : row * columns + half] = even[row]
            state_ref[span, row * columns + half : (row + 1) * columns] = odd[row]
        return carry

    lax.fori_loop(0, levels // SUB, diffuse, 0)

    vert_pad[...] = jnp.zeros_like(vert_pad)
    vert_pad[:depth, :depth] = vert_ref[...]
    factor = vert_pad[...]
    for row in range(out_rows):
        scale = jnp.concatenate([scales[0][row : row + 1], scales[1][row : row + 1]], 1)
        mixed = jnp.dot(
            factor,
            state_ref[:, row * columns : (row + 1) * columns],
            precision=EXACT,
            preferred_element_type=F32,
        )
        field_ref[row * levels : (row + 1) * levels, :] = (mixed * scale).astype(jnp.bfloat16)

    place = iota((columns, 2 * LANES), 0)
    col = jnp.where(place < half, 2 * place, 2 * (place - half) + 1).astype(F32)

    def interpolate(pair, carry):
        tails = [recv_ref[2 * pair + k, 2 * tile_rows :, :] for k in range(2)]
        pos_x = jnp.concatenate([tails[0][2:3], tails[1][2:3]], 1)
        pos_y = jnp.concatenate([tails[0][3:4], tails[1][3:4]], 1)
        hat = jnp.maximum(1.0 - jnp.abs(pos_x - col), 0.0).astype(jnp.bfloat16)
        total = None
        for row in range(out_rows):
            along = jnp.dot(
                field_ref[row * levels : (row + 1) * levels, :], hat, preferred_element_type=F32
            )
            weight = jnp.maximum(1.0 - jnp.abs(pos_y - float(row)), 0.0)
            total = along * weight if total is None else total + along * weight
        rounded = total[:depth].astype(jnp.bfloat16)
        prof_ref[2 * pair] = rounded[:, :LANES]
        prof_ref[2 * pair + 1] = rounded[:, LANES:]
        return carry

    lax.fori_loop(0, tiles // 2, interpolate, 0)


def weave_kernel(field_ref, out_ref, flat_ref):
    depth, tile_rows, columns = out_ref.shape
    levels = field_ref.shape[0] // (tile_rows + 1)
    half = columns // 2
    place = iota((columns, columns), 0)
    col = iota((columns, columns), 1)
    source = jnp.where(place < half, 2 * place, 2 * (place - half) + 1)
    weave = (col == source).astype(jnp.bfloat16)
    for row in range(tile_rows):
        woven = jnp.dot(
            field_ref[row * levels : (row + 1) * levels, :], weave, preferred_element_type=F32
        )
        flat_ref[:, row, :] = woven
    out_ref[...] = flat_ref[:depth].astype(jnp.bfloat16)


def body(
    noise_seeds, diffusivity, wet_mask, vert_factor, norm_scale, obs_cell, obs_frac, obs_count
):
    tile_rows, columns = diffusivity.shape
    depth = vert_factor.shape[0]
    levels = up(depth, 2 * SUB)
    tiles = lax.axis_size("tile")
    total_rows = tile_rows * tiles
    half = columns // 2
    rows = tile_rows + 1 + 2 * STEPS
    slots = obs_cell.shape[2]

    packed, norm_split = pl.pallas_call(
        pack_kernel,
        out_shape=(
            jax.ShapeDtypeStruct((tiles, 2 * tile_rows + SUB, LANES), F32),
            jax.ShapeDtypeStruct((2 * tile_rows, half), F32),
        ),
        in_specs=[VMEM] * 5 + [SMEM],
        out_specs=(VMEM, VMEM),
        name="pack",
    )(diffusivity, wet_mask, norm_scale, obs_cell[0], obs_frac[0], obs_count)
    received = lax.all_to_all(packed, "tile", split_axis=0, concat_axis=0, tiled=True)

    noise = pl.pallas_call(
        lambda *refs: noise_kernel(total_rows, tile_rows, columns, *refs),
        out_shape=pltpu.VMEM((2 * rows, levels, half), F32),
        in_specs=[SMEM],
        out_specs=VMEM,
        name="noise",
        compiler_params=LIMIT,
    )(noise_seeds)

    flat = (2 * rows, SUB, LANES)
    answers, field = pl.pallas_call(
        lambda *refs: field_kernel(tiles, *refs),
        out_shape=(
            jax.ShapeDtypeStruct((tiles, depth, slots), jnp.bfloat16),
            pltpu.VMEM(((tile_rows + 1) * levels, columns), jnp.bfloat16),
        ),
        in_specs=[VMEM] * 4,
        out_specs=(VMEM, VMEM),
        scratch_shapes=[
            pltpu.VMEM((up(rows, SUB), half), F32),
            pltpu.VMEM((up(rows, SUB), half), F32),
            pltpu.VMEM(flat, F32),
            pltpu.VMEM(flat, F32),
            pltpu.VMEM(flat, F32),
            pltpu.VMEM((levels, levels), F32),
            pltpu.VMEM((levels, (tile_rows + 1) * columns), F32),
        ],
        name="field",
        compiler_params=LIMIT,
    )(resident(noise), resident(received), resident(norm_split), vert_factor)
    profiles = lax.all_to_all(answers, "tile", split_axis=0, concat_axis=0, tiled=True)

    perturbation = pl.pallas_call(
        weave_kernel,
        out_shape=jax.ShapeDtypeStruct((depth, tile_rows, columns), jnp.bfloat16),
        in_specs=[VMEM],
        out_specs=VMEM,
        scratch_shapes=[pltpu.VMEM((levels, tile_rows, columns), F32)],
        name="weave",
        compiler_params=LIMIT,
    )(resident(field))
    return (perturbation, profiles[None])


def solution(mesh):
    in_specs = (
        P("member"),
        P("tile", None),
        P("tile", None),
        P(),
        P("tile", None),
        P("tile", None, None),
        P("tile", None, None, None),
        P("tile", None),
    )
    out_specs = (P("member", "tile", None), P("tile", None, "member", None))
    return jax.shard_map(body, mesh=mesh, in_specs=in_specs, out_specs=out_specs, check_vma=False)
```

```python
import jax
import jax.numpy as jnp
from jax import lax
from jax.experimental import pallas as pl
from jax.experimental.pallas import tpu as pltpu
from jax.sharding import PartitionSpec as P

STEPS = 8
LANES = 128
SUB = 8
EXACT = lax.Precision.HIGHEST
F32 = jnp.float32
BF16 = jnp.bfloat16
WAYS = 4
UNROLL = 2
I32 = jnp.int32
GOLDEN = -1640531535
ROOT12 = 3.4641016151377544
VMEM = pl.BlockSpec(memory_space=pltpu.VMEM)
SMEM = pl.BlockSpec(memory_space=pltpu.SMEM)
LIMIT = pltpu.CompilerParams(vmem_limit_bytes=24 << 20)


def resident(array):
    return pltpu.with_memory_space_constraint(array, pltpu.VMEM)


def up(value, unit):
    return -(-value // unit) * unit


def wrapped(value):
    return (value + 2**31) % 2**32 - 2**31


def iota(shape, axis):
    return lax.broadcasted_iota(I32, shape, axis)


def column_of(place, columns):
    run = columns // WAYS
    turn = sum(((place >= k * run).astype(I32) for k in range(1, WAYS)), jnp.zeros_like(place))
    return WAYS * (place - turn * run) + turn


def pack_kernel(
    diff_ref, wet_ref, norm_ref, cell_ref, frac_ref, count_ref, out_ref, kappa_out, norm_out
):
    tile_rows, columns = diff_ref.shape
    owners = cell_ref.shape[0]
    kappa = diff_ref[...] * wet_ref[...].astype(F32)
    square = (columns, columns)
    parting = (iota(square, 0) == column_of(iota(square, 1), columns)).astype(F32)
    both = jnp.concatenate([kappa, norm_ref[...]], 0)
    parted = jnp.dot(both, parting, precision=EXACT, preferred_element_type=F32)
    kappa_out[...] = parted[:tile_rows]
    norm_out[...] = parted[tile_rows:]
    parts = columns // LANES
    halo = jnp.concatenate(
        [parted[:tile_rows, k * LANES : (k + 1) * LANES] for k in range(parts)], 0
    ).astype(BF16)
    norms = [parted[tile_rows : tile_rows + 1, k * LANES : (k + 1) * LANES] for k in range(parts)]
    cell = cell_ref[...]
    row = jnp.zeros_like(cell)
    for step in range(1, tile_rows):
        row = row + (cell >= step * columns).astype(I32)
    col = (cell - row * columns).astype(F32)
    row = row.astype(F32)
    frac_y, frac_x = frac_ref[:, 0, :], frac_ref[:, 1, :]
    high_y, high_x = (frac.astype(BF16).astype(F32) for frac in (frac_y, frac_x))
    low_y, low_x = frac_y - high_y, frac_x - high_x
    lane = iota((1, LANES), 1)
    for owner in range(owners):
        at = slice(owner, owner + 1)
        live = lane < count_ref[0, owner]
        tail = jnp.concatenate(
            norms + [col[at], high_x[at], low_x[at]]
            + [jnp.where(live, row[at], -16.0), high_y[at], low_y[at]],
            0,
        )
        out_ref[owner, : parts * tile_rows, :] = halo
        out_ref[owner, parts * tile_rows :, :] = tail.astype(BF16)


def mix(hashed):
    hashed = (hashed ^ lax.shift_right_logical(hashed, 16)) * -2048144789
    hashed = (hashed ^ lax.shift_right_logical(hashed, 13)) * -1028477387
    hashed = hashed ^ lax.shift_right_logical(hashed, 16)
    return hashed


def noise_kernel(total_rows, tile_rows, columns, seed_ref, out_ref):
    planes, height, _ = out_ref.shape
    run = columns // WAYS
    groups = LANES // run
    first_row = lax.axis_index("tile") * tile_rows - STEPS
    step_level = wrapped(total_rows * columns * GOLDEN)
    shape = (SUB, LANES)
    group = sum(((iota(shape, 1) >= g * run).astype(I32) for g in range(1, groups)), 0)
    base = (iota(shape, 0) + SUB * group) * step_level
    base = base + (iota(shape, 1) - group * run) * wrapped(WAYS * GOLDEN)
    gain = ROOT12 / 16777216.0
    shift = (0.5 / 16777216.0 - 0.5) * ROOT12
    origin = first_row * wrapped(columns * GOLDEN) + seed_ref[0]
    second = seed_ref[1]

    def one_tile(part, carry):
        start = origin + part * wrapped(groups * SUB * step_level)
        span = pl.ds(pl.multiple_of(part * SUB, SUB), SUB)
        for plane in range(planes):
            offset = start + wrapped(((plane // WAYS) * columns + plane % WAYS) * GOLDEN)
            hashed = mix(mix(base + offset) ^ second)
            drawn = lax.shift_right_logical(hashed, 8).astype(F32)
            out_ref[plane, span, :] = drawn * gain + shift
        return carry

    lax.fori_loop(0, height // SUB, one_tile, 0)


def field_kernel(
    tiles, noise_ref, recv_ref, kappa_ref, norm_ref, vert_ref, prof_ref, field_ref,
    halo_ref, root_ref, keep_ref, gain_ref, vert_pad, state_ref,
):
    planes, height, _ = noise_ref.shape
    rows = planes // WAYS
    tile_rows, columns = norm_ref.shape
    run = columns // WAYS
    groups = LANES // run
    levels = height * groups
    depth = vert_ref.shape[0]
    out_rows = tile_rows + 1
    parts = columns // LANES
    tile = lax.axis_index("tile")

    halo_ref[...] = jnp.zeros_like(halo_ref)
    halo_ref[tile_rows : 2 * tile_rows] = kappa_ref[...]
    for place, shift, count in ((0, -1, tile_rows), (2, 1, tile_rows), (3, 2, 1)):
        source = tile + shift
        valid = ((source >= 0) & (source < tiles)).astype(F32)
        given = recv_ref[jnp.clip(source, 0, tiles - 1), : parts * tile_rows, :].astype(F32) * valid
        for k in range(parts):
            halo_ref[place * tile_rows : place * tile_rows + count, k * LANES : (k + 1) * LANES] = (
                given[k * tile_rows : k * tile_rows + count]
            )
    root = jnp.sqrt(halo_ref[...])
    lane = iota((1, LANES), 1)
    roots = []
    for k in range(WAYS):
        vector = root[:, (k // groups) * LANES : (k // groups + 1) * LANES]
        turned = pltpu.roll(vector, run, 1)
        keeps = (lane >= run) if k % groups else (lane < run)
        roots.append(jnp.where(keeps, vector, turned))
        root_ref[k] = roots[k]
    edge_low, edge_high = (lane == 0) | (lane == run), (lane == run - 1) | (lane == LANES - 1)
    inner = slice(1, rows - 1)
    for k in range(WAYS):
        west = roots[k - 1] if k else jnp.where(edge_low, 0.0, pltpu.roll(roots[-1], 1, 1))
        east = (
            roots[k + 1]
            if k < WAYS - 1
            else jnp.where(edge_high, 0.0, pltpu.roll(roots[0], LANES - 1, 1))
        )
        near = root_ref[k, : rows - 2] + root_ref[k, 2:rows] + (west + east)[inner]
        keep_ref[k, inner] = 1.0 - roots[k][inner] * near
        gain_ref[k, inner] = roots[k][inner] * roots[k][inner]
    kappa = halo_ref[STEPS : STEPS + out_rows]
    wet = kappa > 0.0
    inverse = jnp.where(wet, root[STEPS : STEPS + out_rows] / jnp.where(wet, kappa, 1.0), 0.0)
    below = recv_ref[jnp.clip(tile + 1, 0, tiles - 1), parts * tile_rows :, :].astype(F32)
    norm_below = jnp.concatenate([below[k : k + 1] for k in range(parts)], 1)
    scales = inverse * jnp.concatenate([norm_ref[...], norm_below], 0)

    block = (SUB, LANES)
    lanes = iota(block, 1)
    low8, high8 = (lanes == 0) | (lanes == run), (lanes == run - 1) | (lanes == LANES - 1)
    lower = lanes < run

    def spread(ref, k, row):
        return ref[k, pl.ds(row, SUB, stride=0), :]

    def diffuse(part, carry):
        span = pl.ds(pl.multiple_of(part * SUB, SUB), SUB)
        out_span = pl.ds(pl.multiple_of(part * groups * SUB, groups * SUB), groups * SUB)
        low_span = pl.ds(pl.multiple_of(levels + part * groups * SUB, groups * SUB), groups * SUB)
        again = pl.ds(pl.multiple_of(2 * levels + part * groups * SUB, groups * SUB), groups * SUB)
        known = [{} for _ in range(STEPS + 1)]
        for top in range(rows):
            known[0][top] = [
                noise_ref[WAYS * top + k, span, :] * spread(root_ref, k, top) for k in range(WAYS)
            ]
            for step in range(1, STEPS + 1):
                row = top - step
                if row < step:
                    break
                past = known[step - 1]
                here = past[row]
                fresh = []
                for k in range(WAYS):
                    west = here[k - 1] if k else jnp.where(low8, 0.0, pltpu.roll(here[-1], 1, 1))
                    east = (
                        here[k + 1]
                        if k < WAYS - 1
                        else jnp.where(high8, 0.0, pltpu.roll(here[0], LANES - 1, 1))
                    )
                    near = (past[row - 1][k] + past[row + 1][k]) + (west + east)
                    fresh.append(spread(keep_ref, k, row) * here[k] + spread(gain_ref, k, row) * near)
                known[step][row] = fresh
                del past[row - 1]
        for row in range(out_rows):
            done = known[STEPS][STEPS + row]
            for k in range(parts):
                one, two = done[2 * k], done[2 * k + 1]
                low = jnp.where(lower, one, pltpu.roll(two, run, 1))
                high = jnp.where(lower, pltpu.roll(one, run, 1), two)
                state = jnp.concatenate([low, high], 0)
                head = state.astype(BF16)
                at = slice(row * columns + k * LANES, row * columns + (k + 1) * LANES)
                state_ref[out_span, at] = head
                state_ref[low_span, at] = (state - head.astype(F32)).astype(BF16)
                state_ref[again, at] = head
        return carry

    lax.fori_loop(0, height // SUB, diffuse, 0)

    vert_pad[...] = jnp.zeros_like(vert_pad)
    vert_pad[:depth, :depth] = vert_ref[...]
    vert = vert_pad[...]
    head = vert.astype(BF16).astype(F32)
    factor = head + pltpu.roll(head, levels, 1) + pltpu.roll(vert - head, 2 * levels, 1)
    factor = factor.astype(BF16)[:, : 3 * levels]
    for row in range(out_rows):
        mixed = jnp.dot(
            factor,
            state_ref[:, row * columns : (row + 1) * columns],
            preferred_element_type=F32,
        )
        scaled = (mixed * scales[row : row + 1]).astype(BF16)
        field_ref[row * levels : (row + 1) * levels, :] = scaled

    col = column_of(iota((columns, 2 * LANES), 0), columns).astype(F32)

    def interpolate(pair, carry):
        tails = [recv_ref[2 * pair + k, parts * tile_rows :, :].astype(F32) for k in range(2)]
        tail = jnp.concatenate(tails, 1)
        pos_x = tail[parts : parts + 1] + (tail[parts + 1 : parts + 2] + tail[parts + 2 : parts + 3])
        pos_y = tail[parts + 3 : parts + 4] + (tail[parts + 4 : parts + 5] + tail[parts + 5 : parts + 6])
        hat = jnp.maximum(1.0 - jnp.abs(pos_x - col), 0.0).astype(BF16)
        total = None
        for row in range(out_rows):
            along = jnp.dot(
                field_ref[row * levels : (row + 1) * levels, :], hat, preferred_element_type=F32
            )
            weight = jnp.maximum(1.0 - jnp.abs(pos_y - float(row)), 0.0)
            total = along * weight if total is None else total + along * weight
        rounded = total[:depth].astype(BF16)
        prof_ref[2 * pair] = rounded[:, :LANES]
        prof_ref[2 * pair + 1] = rounded[:, LANES:]
        return carry

    lax.fori_loop(0, tiles // 2, interpolate, 0, unroll=UNROLL)


def weave_kernel(field_ref, out_ref, flat_ref):
    depth, tile_rows, columns = out_ref.shape
    levels = field_ref.shape[0] // (tile_rows + 1)
    square = (columns, columns)
    weave = (iota(square, 1) == column_of(iota(square, 0), columns)).astype(BF16)
    for row in range(tile_rows):
        woven = jnp.dot(
            field_ref[row * levels : (row + 1) * levels, :], weave, preferred_element_type=F32
        )
        flat_ref[:, row, :] = woven
    out_ref[...] = flat_ref[:depth].astype(BF16)


def body(
    noise_seeds, diffusivity, wet_mask, vert_factor, norm_scale, obs_cell, obs_frac, obs_count
):
    tile_rows, columns = diffusivity.shape
    depth = vert_factor.shape[0]
    levels = up(depth, 2 * SUB)
    tiles = lax.axis_size("tile")
    total_rows = tile_rows * tiles
    groups = LANES * WAYS // columns
    rows = tile_rows + 1 + 2 * STEPS
    slots = obs_cell.shape[2]
    parts = columns // LANES
    square = jax.ShapeDtypeStruct((tile_rows, columns), F32)

    packed, kappa_split, norm_split = pl.pallas_call(
        pack_kernel,
        out_shape=(
            jax.ShapeDtypeStruct((tiles, parts * tile_rows + SUB, LANES), BF16),
            square,
            square,
        ),
        in_specs=[VMEM] * 5 + [SMEM],
        out_specs=(VMEM,) * 3,
        name="pack",
    )(diffusivity, wet_mask, norm_scale, obs_cell[0], obs_frac[0], obs_count)
    received = lax.all_to_all(packed, "tile", split_axis=0, concat_axis=0, tiled=True)

    noise = pl.pallas_call(
        lambda *refs: noise_kernel(total_rows, tile_rows, columns, *refs),
        out_shape=pltpu.VMEM((WAYS * rows, levels // groups, LANES), F32),
        in_specs=[SMEM],
        out_specs=VMEM,
        name="noise",
        compiler_params=LIMIT,
    )(noise_seeds)

    coefficients = pltpu.VMEM((WAYS, up(rows, SUB), LANES), F32)
    answers, field = pl.pallas_call(
        lambda *refs: field_kernel(tiles, *refs),
        out_shape=(
            jax.ShapeDtypeStruct((tiles, depth, slots), BF16),
            pltpu.VMEM(((tile_rows + 1) * levels, columns), BF16),
        ),
        in_specs=[VMEM] * 5,
        out_specs=(VMEM, VMEM),
        scratch_shapes=[
            pltpu.VMEM((up(rows, SUB), columns), F32),
            coefficients,
            coefficients,
            coefficients,
            pltpu.VMEM((levels, up(3 * levels, LANES)), F32),
            pltpu.VMEM((3 * levels, (tile_rows + 1) * columns), BF16),
        ],
        name="field",
        compiler_params=LIMIT,
    )(resident(noise), resident(received), resident(kappa_split), resident(norm_split), vert_factor)
    profiles = lax.all_to_all(answers, "tile", split_axis=0, concat_axis=0, tiled=True)

    perturbation = pl.pallas_call(
        weave_kernel,
        out_shape=jax.ShapeDtypeStruct((depth, tile_rows, columns), BF16),
        in_specs=[VMEM],
        out_specs=VMEM,
        scratch_shapes=[pltpu.VMEM((levels, tile_rows, columns), F32)],
        name="weave",
        compiler_params=LIMIT,
    )(resident(field))
    return (perturbation, profiles[None])


def solution(mesh):
    in_specs = (
        P("member"),
        P("tile", None),
        P("tile", None),
        P(),
        P("tile", None),
        P("tile", None, None),
        P("tile", None, None, None),
        P("tile", None),
    )
    out_specs = (P("member", "tile", None), P("tile", None, "member", None))
    return jax.shard_map(body, mesh=mesh, in_specs=in_specs, out_specs=out_specs, check_vma=False)
```

```python
import jax
import jax.numpy as jnp
from jax import lax
from jax.experimental import pallas as pl
from jax.experimental.pallas import tpu as pltpu
from jax.sharding import PartitionSpec as P

STEPS = 8
LANES = 128
SUB = 8
EXACT = lax.Precision.HIGHEST
F32 = jnp.float32
BF16 = jnp.bfloat16
WAYS = 4
TOGETHER = 5
PAIRS = 8
I32 = jnp.int32
GOLDEN = -1640531535
ROOT12 = 3.4641016151377544
VMEM = pl.BlockSpec(memory_space=pltpu.VMEM)
SMEM = pl.BlockSpec(memory_space=pltpu.SMEM)
LIMIT = pltpu.CompilerParams(vmem_limit_bytes=24 << 20)


def resident(array):
    return pltpu.with_memory_space_constraint(array, pltpu.VMEM)


def up(value, unit):
    return -(-value // unit) * unit


def wrapped(value):
    return (value + 2**31) % 2**32 - 2**31


def iota(shape, axis):
    return lax.broadcasted_iota(I32, shape, axis)


def visiting_order(tiles):
    pairs = tiles // 2
    ring = list(range(1, pairs, 2)) + list(range(0, pairs, 2))[::-1]
    turn = pairs // 4
    return [2 * pair + core for pair in ring[turn:] + ring[:turn] for core in (1, 0)]


def place_of(tile, tiles):
    order = visiting_order(tiles)
    return sum(jnp.where(tile == order[place], place, 0) for place in range(1, tiles))


def column_of(place, columns):
    run = columns // WAYS
    turn = sum(((place >= k * run).astype(I32) for k in range(1, WAYS)), jnp.zeros_like(place))
    return WAYS * (place - turn * run) + turn


def pack_kernel(
    diff_ref, wet_ref, norm_ref, cell_ref, frac_ref, count_ref, out_ref, kappa_out, norm_out
):
    tile_rows, columns = diff_ref.shape
    owners = cell_ref.shape[0]
    order = visiting_order(owners)
    kappa = diff_ref[...] * wet_ref[...].astype(F32)
    square = (columns, columns)
    parting = (iota(square, 0) == column_of(iota(square, 1), columns)).astype(F32)
    both = jnp.concatenate([kappa, norm_ref[...]], 0)
    parted = jnp.dot(both, parting, precision=EXACT, preferred_element_type=F32)
    kappa_out[...] = parted[:tile_rows]
    norm_out[...] = parted[tile_rows:]
    parts = columns // LANES
    halo = jnp.concatenate(
        [parted[:tile_rows, k * LANES : (k + 1) * LANES] for k in range(parts)], 0
    ).astype(BF16)
    norms = [parted[tile_rows : tile_rows + 1, k * LANES : (k + 1) * LANES] for k in range(parts)]
    cell = cell_ref[...]
    row = jnp.zeros_like(cell)
    for step in range(1, tile_rows):
        row = row + (cell >= step * columns).astype(I32)
    col = (cell - row * columns).astype(F32)
    row = row.astype(F32)
    frac_y, frac_x = frac_ref[:, 0, :], frac_ref[:, 1, :]
    high_y, high_x = (frac.astype(BF16).astype(F32) for frac in (frac_y, frac_x))
    low_y, low_x = frac_y - high_y, frac_x - high_x
    lane = iota((1, LANES), 1)
    for owner in range(owners):
        at = slice(owner, owner + 1)
        live = lane < count_ref[0, owner]
        tail = jnp.concatenate(
            norms + [col[at], high_x[at], low_x[at]]
            + [jnp.where(live, row[at], -16.0), high_y[at], low_y[at]],
            0,
        )
        at = order.index(owner)
        out_ref[at, : parts * tile_rows, :] = halo
        out_ref[at, parts * tile_rows :, :] = tail.astype(BF16)


def mix(hashed):
    hashed = (hashed ^ lax.shift_right_logical(hashed, 16)) * -2048144789
    hashed = (hashed ^ lax.shift_right_logical(hashed, 13)) * -1028477387
    hashed = hashed ^ lax.shift_right_logical(hashed, 16)
    return hashed


def noise_kernel(total_rows, tile_rows, columns, seed_ref, out_ref):
    planes, height, _ = out_ref.shape
    run = columns // WAYS
    groups = LANES // run
    first_row = lax.axis_index("tile") * tile_rows - STEPS
    step_level = wrapped(total_rows * columns * GOLDEN)
    shape = (SUB, LANES)
    group = sum(((iota(shape, 1) >= g * run).astype(I32) for g in range(1, groups)), 0)
    base = (iota(shape, 0) + SUB * group) * step_level
    base = base + (iota(shape, 1) - group * run) * wrapped(WAYS * GOLDEN)
    gain = ROOT12 / 16777216.0
    shift = (0.5 / 16777216.0 - 0.5) * ROOT12
    origin = first_row * wrapped(columns * GOLDEN) + seed_ref[0]
    second = seed_ref[1]

    def one_tile(part, carry):
        start = origin + part * wrapped(groups * SUB * step_level)
        span = pl.ds(pl.multiple_of(part * SUB, SUB), SUB)
        for plane in range(planes):
            offset = start + wrapped(((plane // WAYS) * columns + plane % WAYS) * GOLDEN)
            hashed = mix(mix(base + offset) ^ second)
            drawn = lax.shift_right_logical(hashed, 8).astype(F32)
            out_ref[plane, span, :] = drawn * gain + shift
        return carry

    lax.fori_loop(0, height // SUB, one_tile, 0)


def field_kernel(
    tiles, noise_ref, recv_ref, kappa_ref, norm_ref, vert_ref, prof_ref, field_ref,
    halo_ref, root_ref, keep_ref, gain_ref, vert_pad, state_ref, hat_ref,
):
    planes, height, _ = noise_ref.shape
    rows = planes // WAYS
    tile_rows, columns = norm_ref.shape
    run = columns // WAYS
    groups = LANES // run
    levels = height * groups
    depth = vert_ref.shape[0]
    out_rows = tile_rows + 1
    parts = columns // LANES
    tile = lax.axis_index("tile")

    halo_ref[...] = jnp.zeros_like(halo_ref)
    halo_ref[tile_rows : 2 * tile_rows] = kappa_ref[...]
    for place, shift, count in ((0, -1, tile_rows), (2, 1, tile_rows), (3, 2, 1)):
        source = tile + shift
        valid = ((source >= 0) & (source < tiles)).astype(F32)
        given = recv_ref[place_of(jnp.clip(source, 0, tiles - 1), tiles), : parts * tile_rows, :].astype(F32) * valid
        for k in range(parts):
            halo_ref[place * tile_rows : place * tile_rows + count, k * LANES : (k + 1) * LANES] = (
                given[k * tile_rows : k * tile_rows + count]
            )
    root = jnp.sqrt(halo_ref[...])
    lane = iota((1, LANES), 1)
    roots = []
    for k in range(WAYS):
        vector = root[:, (k // groups) * LANES : (k // groups + 1) * LANES]
        turned = pltpu.roll(vector, run, 1)
        keeps = (lane >= run) if k % groups else (lane < run)
        roots.append(jnp.where(keeps, vector, turned))
        root_ref[k] = roots[k]
    edge_low, edge_high = (lane == 0) | (lane == run), (lane == run - 1) | (lane == LANES - 1)
    inner = slice(1, rows - 1)
    for k in range(WAYS):
        west = roots[k - 1] if k else jnp.where(edge_low, 0.0, pltpu.roll(roots[-1], 1, 1))
        east = (
            roots[k + 1]
            if k < WAYS - 1
            else jnp.where(edge_high, 0.0, pltpu.roll(roots[0], LANES - 1, 1))
        )
        near = root_ref[k, : rows - 2] + root_ref[k, 2:rows] + (west + east)[inner]
        keep_ref[k, inner] = 1.0 - roots[k][inner] * near
        gain_ref[k, inner] = roots[k][inner] * roots[k][inner]
    kappa = halo_ref[STEPS : STEPS + out_rows]
    wet = kappa > 0.0
    inverse = jnp.where(wet, root[STEPS : STEPS + out_rows] / jnp.where(wet, kappa, 1.0), 0.0)
    below = recv_ref[place_of(jnp.clip(tile + 1, 0, tiles - 1), tiles), parts * tile_rows :, :].astype(F32)
    norm_below = jnp.concatenate([below[k : k + 1] for k in range(parts)], 1)
    scales = inverse * jnp.concatenate([norm_ref[...], norm_below], 0)

    block = (SUB, LANES)
    lanes = iota(block, 1)
    low8, high8 = (lanes == 0) | (lanes == run), (lanes == run - 1) | (lanes == LANES - 1)
    lower = lanes < run

    def spread(ref, k, row):
        return ref[k, pl.ds(row, SUB, stride=0), :]

    def diffuse(bundle, carry):
        spans = [
            pl.ds(pl.multiple_of((bundle * TOGETHER + part) * SUB, SUB), SUB) for part in range(TOGETHER)
        ]
        known = [{} for _ in range(STEPS + 1)]

        def drawn(row):
            cells = []
            for k in range(WAYS):
                scale = spread(root_ref, k, row)
                cells.append([noise_ref[WAYS * row + k, span, :] * scale for span in spans])
            return cells

        def stepped(past, row):
            here, fresh = past[row], []
            for k in range(WAYS):
                keep, gain = spread(keep_ref, k, row), spread(gain_ref, k, row)
                cells = []
                for part in range(TOGETHER):
                    if k:
                        west = here[k - 1][part]
                    else:
                        west = jnp.where(low8, 0.0, pltpu.roll(here[-1][part], 1, 1))
                    if k < WAYS - 1:
                        east = here[k + 1][part]
                    else:
                        east = jnp.where(high8, 0.0, pltpu.roll(here[0][part], LANES - 1, 1))
                    near = (past[row - 1][k][part] + past[row + 1][k][part]) + (west + east)
                    cells.append(keep * here[k][part] + gain * near)
                fresh.append(cells)
            return fresh

        for top in range(rows):
            known[0][top] = drawn(top)
            for step in range(1, STEPS + 1):
                row = top - step
                if row < step:
                    break
                known[step][row] = stepped(known[step - 1], row)
                del known[step - 1][row - 1]
        for row in range(out_rows):
            done = known[STEPS][row + STEPS]
            for k in range(parts):
                for part in range(TOGETHER):
                    one, two = done[2 * k][part], done[2 * k + 1][part]
                    low = jnp.where(lower, one, pltpu.roll(two, run, 1))
                    high = jnp.where(lower, pltpu.roll(one, run, 1), two)
                    state = jnp.concatenate([low, high], 0)
                    head = state.astype(BF16)
                    tail = (state - head.astype(F32)).astype(BF16)
                    first = row * columns + k * LANES
                    for place, piece in enumerate((head, tail, head)):
                        start = place * levels + (bundle * TOGETHER + part) * 2 * SUB
                        at = pl.ds(pl.multiple_of(start, 2 * SUB), 2 * SUB)
                        state_ref[at, first : first + LANES] = piece
        return carry

    lax.fori_loop(0, height // SUB // TOGETHER, diffuse, 0)

    vert_pad[...] = jnp.zeros_like(vert_pad)
    vert_pad[:depth, :depth] = vert_ref[...]
    vert = vert_pad[...]
    head = vert.astype(BF16).astype(F32)
    factor = head + pltpu.roll(head, levels, 1) + pltpu.roll(vert - head, 2 * levels, 1)
    factor = factor.astype(BF16)[:, : 3 * levels]
    bunch = 2 * SUB
    for row in range(out_rows):
        mixed = jnp.dot(
            factor,
            state_ref[:, row * columns : (row + 1) * columns],
            preferred_element_type=F32,
        )
        scaled = (mixed * scales[row : row + 1]).astype(BF16)
        for part in range(levels // bunch):
            first = (part * out_rows + row) * bunch
            field_ref[first : first + bunch, :] = scaled[part * bunch : (part + 1) * bunch]

    col = column_of(iota((columns, 2 * LANES), 0), columns).astype(F32)

    def positions(pair, first):
        tails = [recv_ref[2 * pair + k, parts * tile_rows :, :].astype(F32) for k in range(2)]
        tail = jnp.concatenate(tails, 1)
        return tail[first : first + 1] + (tail[first + 1 : first + 2] + tail[first + 2 : first + 3])

    def make_hat(pair, slot):
        hat_ref[slot] = jnp.maximum(1.0 - jnp.abs(positions(pair, parts) - col), 0.0).astype(BF16)

    def answer(pair, hat):
        along = jnp.dot(field_ref[...], hat, preferred_element_type=F32)
        pos_y = positions(pair, parts + 3)
        weights = [jnp.maximum(1.0 - jnp.abs(pos_y - float(row)), 0.0) for row in range(out_rows)]
        for part in range(levels // bunch):
            total = None
            for row in range(out_rows):
                first = (part * out_rows + row) * bunch
                term = along[first : first + bunch] * weights[row]
                total = term if total is None else total + term
            kept = min(bunch, depth - part * bunch)
            rounded = total.astype(BF16)[:kept]
            prof_ref[2 * pair, part * bunch : part * bunch + kept, :] = rounded[:, :LANES]
            prof_ref[2 * pair + 1, part * bunch : part * bunch + kept, :] = rounded[:, LANES:]

    def some_pairs(step, carry):
        for slot in range(PAIRS):
            make_hat(step * PAIRS + slot, slot)
        for slot in range(PAIRS):
            answer(step * PAIRS + slot, hat_ref[slot])
        return carry

    lax.fori_loop(0, tiles // (2 * PAIRS), some_pairs, 0)


def weave_kernel(field_ref, out_ref, flat_ref):
    depth, tile_rows, columns = out_ref.shape
    levels = field_ref.shape[0] // (tile_rows + 1)
    square = (columns, columns)
    weave = (iota(square, 1) == column_of(iota(square, 0), columns)).astype(BF16)
    woven = jnp.dot(field_ref[...], weave, preferred_element_type=F32)
    bunch = 2 * SUB
    for part in range(levels // bunch):
        for row in range(tile_rows):
            first = (part * (tile_rows + 1) + row) * bunch
            flat_ref[part * bunch : (part + 1) * bunch, row, :] = woven[first : first + bunch]
    out_ref[...] = flat_ref[:depth].astype(BF16)


def unpack_kernel(order, given_ref, out_ref, wide_ref, ready_ref, sems):
    depth = given_ref.shape[1]
    bunch = 2 * SUB
    copies = []
    for part, start in enumerate(range(0, depth, bunch)):
        stop = min(start + bunch, depth)
        for place, owner in enumerate(order):
            wide_ref[start:stop, owner, :] = given_ref[place, start:stop, :].astype(F32)
        ready_ref[start:stop] = wide_ref[start:stop].astype(BF16)
        copies.append(
            pltpu.make_async_copy(ready_ref.at[start:stop], out_ref.at[start:stop], sems.at[part])
        )
        copies[-1].start()
    for copy in copies:
        copy.wait()


def body(
    noise_seeds, diffusivity, wet_mask, vert_factor, norm_scale, obs_cell, obs_frac, obs_count
):
    tile_rows, columns = diffusivity.shape
    depth = vert_factor.shape[0]
    levels = up(depth, 2 * SUB)
    tiles = lax.axis_size("tile")
    total_rows = tile_rows * tiles
    groups = LANES * WAYS // columns
    rows = tile_rows + 1 + 2 * STEPS
    slots = obs_cell.shape[2]
    parts = columns // LANES
    square = jax.ShapeDtypeStruct((tile_rows, columns), F32)

    packed, kappa_split, norm_split = pl.pallas_call(
        pack_kernel,
        out_shape=(
            jax.ShapeDtypeStruct((tiles, parts * tile_rows + SUB, LANES), BF16),
            square,
            square,
        ),
        in_specs=[VMEM] * 5 + [SMEM],
        out_specs=(VMEM,) * 3,
        name="pack",
    )(diffusivity, wet_mask, norm_scale, obs_cell[0], obs_frac[0], obs_count)
    order = visiting_order(tiles)
    exchange = dict(
        axis_name="tile", split_axis=0, concat_axis=0, tiled=True, axis_index_groups=[order]
    )
    received = lax.all_to_all(packed, **exchange)

    noise = pl.pallas_call(
        lambda *refs: noise_kernel(total_rows, tile_rows, columns, *refs),
        out_shape=pltpu.VMEM((WAYS * rows, levels // groups, LANES), F32),
        in_specs=[SMEM],
        out_specs=VMEM,
        name="noise",
        compiler_params=LIMIT,
    )(noise_seeds)

    coefficients = pltpu.VMEM((WAYS, up(rows, SUB), LANES), F32)
    answers, field = pl.pallas_call(
        lambda *refs: field_kernel(tiles, *refs),
        out_shape=(
            jax.ShapeDtypeStruct((tiles, depth, slots), BF16),
            pltpu.VMEM(((tile_rows + 1) * levels, columns), BF16),
        ),
        in_specs=[VMEM] * 5,
        out_specs=(VMEM, VMEM),
        scratch_shapes=[
            pltpu.VMEM((up(rows, SUB), columns), F32),
            coefficients,
            coefficients,
            coefficients,
            pltpu.VMEM((levels, up(3 * levels, LANES)), F32),
            pltpu.VMEM((3 * levels, (tile_rows + 1) * columns), BF16),
            pltpu.VMEM((PAIRS, columns, 2 * LANES), BF16),
        ],
        name="field",
        compiler_params=LIMIT,
    )(resident(noise), resident(received), resident(kappa_split), resident(norm_split), vert_factor)
    gathered = lax.all_to_all(answers, **exchange)
    perturbation = pl.pallas_call(
        weave_kernel,
        out_shape=jax.ShapeDtypeStruct((depth, tile_rows, columns), BF16),
        in_specs=[VMEM],
        out_specs=VMEM,
        scratch_shapes=[pltpu.VMEM((levels, tile_rows, columns), F32)],
        name="weave",
        compiler_params=LIMIT,
    )(resident(field))
    chunks = levels // (2 * SUB)
    profiles = pl.pallas_call(
        lambda *refs: unpack_kernel(order, *refs),
        out_shape=jax.ShapeDtypeStruct((depth, tiles, slots), BF16),
        in_specs=[VMEM],
        out_specs=pl.BlockSpec(memory_space=pl.ANY),
        scratch_shapes=[
            pltpu.VMEM((levels, tiles, slots), F32),
            pltpu.VMEM((levels, tiles, slots), BF16),
            pltpu.SemaphoreType.DMA((chunks,)),
        ],
        name="unpack",
        compiler_params=LIMIT,
    )(resident(gathered))
    return (perturbation, jnp.transpose(profiles, (1, 0, 2))[None])


def solution(mesh):
    in_specs = (
        P("member"),
        P("tile", None),
        P("tile", None),
        P(),
        P("tile", None),
        P("tile", None, None),
        P("tile", None, None, None),
        P("tile", None),
    )
    out_specs = (P("member", "tile", None), P("tile", None, "member", None))
    return jax.shard_map(body, mesh=mesh, in_specs=in_specs, out_specs=out_specs, check_vma=False)
```

```python
import jax
import jax.numpy as jnp
from jax import lax
from jax.experimental import pallas as pl
from jax.experimental.pallas import tpu as pltpu
from jax.sharding import PartitionSpec as P

STEPS = 8
LANES = 128
SUB = 8
EXACT = lax.Precision.HIGHEST
F32 = jnp.float32
BF16 = jnp.bfloat16
WAYS = 4
TOGETHER = 5
PAIRS = 8
SENT = 2
QUAD = 4
I32 = jnp.int32
GOLDEN = -1640531535
ROOT12 = 3.4641016151377544
VMEM = pl.BlockSpec(memory_space=pltpu.VMEM)
SMEM = pl.BlockSpec(memory_space=pltpu.SMEM)
ANY = pl.BlockSpec(memory_space=pl.ANY)
LIMIT = pltpu.CompilerParams(vmem_limit_bytes=24 << 20)


def resident(array):
    return pltpu.with_memory_space_constraint(array, pltpu.VMEM)


def distant(array):
    return pltpu.with_memory_space_constraint(array, pltpu.HBM)


def up(value, unit):
    return -(-value // unit) * unit


def wrapped(value):
    return (value + 2**31) % 2**32 - 2**31


def iota(shape, axis):
    return lax.broadcasted_iota(I32, shape, axis)


def visiting_order(tiles):
    pairs = tiles // 2
    ring = list(range(1, pairs, 2)) + list(range(0, pairs, 2))[::-1]
    turn = pairs // 4
    return [2 * pair + core for pair in ring[turn:] + ring[:turn] for core in (1, 0)]


def place_of(tile, tiles):
    order = visiting_order(tiles)
    return sum(jnp.where(tile == order[place], place, 0) for place in range(1, tiles))


def column_of(place, columns):
    run = columns // WAYS
    turn = sum(((place >= k * run).astype(I32) for k in range(1, WAYS)), jnp.zeros_like(place))
    return WAYS * (place - turn * run) + turn


def pack_kernel(
    diff_ref, wet_ref, norm_ref, cell_ref, frac_ref, count_ref, out_ref, kappa_out, norm_out
):
    tile_rows, columns = diff_ref.shape
    owners = cell_ref.shape[0]
    order = visiting_order(owners)
    kappa = diff_ref[...] * wet_ref[...].astype(F32)
    square = (columns, columns)
    parting = (iota(square, 0) == column_of(iota(square, 1), columns)).astype(F32)
    both = jnp.concatenate([kappa, norm_ref[...]], 0)
    parted = jnp.dot(both, parting, precision=EXACT, preferred_element_type=F32)
    kappa_out[...] = parted[:tile_rows]
    norm_out[...] = parted[tile_rows:]
    parts = columns // LANES
    halo = jnp.concatenate(
        [parted[:tile_rows, k * LANES : (k + 1) * LANES] for k in range(parts)], 0
    ).astype(BF16)
    norms = [parted[tile_rows : tile_rows + 1, k * LANES : (k + 1) * LANES] for k in range(parts)]
    cell = cell_ref[...]
    row = jnp.zeros_like(cell)
    for step in range(1, tile_rows):
        row = row + (cell >= step * columns).astype(I32)
    col = (cell - row * columns).astype(F32)
    row = row.astype(F32)
    frac_y, frac_x = frac_ref[:, 0, :], frac_ref[:, 1, :]
    high_y, high_x = (frac.astype(BF16).astype(F32) for frac in (frac_y, frac_x))
    low_y, low_x = frac_y - high_y, frac_x - high_x
    lane = iota((1, LANES), 1)
    for owner in range(owners):
        at = slice(owner, owner + 1)
        live = lane < count_ref[0, owner]
        tail = jnp.concatenate(
            norms + [col[at], high_x[at], low_x[at]]
            + [jnp.where(live, row[at], -16.0), high_y[at], low_y[at]],
            0,
        )
        at = order.index(owner)
        out_ref[at, : parts * tile_rows, :] = halo
        out_ref[at, parts * tile_rows :, :] = tail.astype(BF16)


def mix(hashed):
    hashed = (hashed ^ lax.shift_right_logical(hashed, 16)) * -2048144789
    hashed = (hashed ^ lax.shift_right_logical(hashed, 13)) * -1028477387
    hashed = hashed ^ lax.shift_right_logical(hashed, 16)
    return hashed


def spread(ref, k, row):
    return ref[k, pl.ds(row, SUB, stride=0), :]


def couple(root, rows, root_ref, keep_ref, gain_ref):
    run = root.shape[1] // WAYS
    groups = LANES // run
    lane = iota((1, LANES), 1)
    roots = []
    for k in range(WAYS):
        vector = root[:, (k // groups) * LANES : (k // groups + 1) * LANES]
        turned = pltpu.roll(vector, run, 1)
        keeps = (lane >= run) if k % groups else (lane < run)
        roots.append(jnp.where(keeps, vector, turned))
        root_ref[k] = roots[k]
    low, high = (lane == 0) | (lane == run), (lane == run - 1) | (lane == LANES - 1)
    inner = slice(1, rows - 1)
    west = [jnp.where(low, 0.0, pltpu.roll(roots[-1], 1, 1))] + roots[:-1]
    east = roots[1:] + [jnp.where(high, 0.0, pltpu.roll(roots[0], LANES - 1, 1))]
    for k in range(WAYS):
        near = root_ref[k, : rows - 2] + root_ref[k, 2:rows] + (west[k] + east[k])[inner]
        keep_ref[k, inner] = 1.0 - roots[k][inner] * near
        gain_ref[k, inner] = roots[k][inner] * roots[k][inner]


def step_on(above, here, under, keep, gain, run):
    lanes = iota((SUB, LANES), 1)
    low, high = (lanes == 0) | (lanes == run), (lanes == run - 1) | (lanes == LANES - 1)
    west = [jnp.where(low, 0.0, pltpu.roll(here[-1], 1, 1))] + here[:-1]
    east = here[1:] + [jnp.where(high, 0.0, pltpu.roll(here[0], LANES - 1, 1))]
    return [
        keep[k] * here[k] + gain[k] * ((above[k] + under[k]) + (west[k] + east[k]))
        for k in range(WAYS)
    ]


def early_rows(tile_rows):
    steps = range(1, min(STEPS, (tile_rows - 1) // 2) + 1)
    return [(step, row) for step in steps for row in range(step, tile_rows - step)]


def noise_kernel(
    total_rows, tile_rows, columns, seed_ref, kappa_ref, norm_ref, vert_ref,
    out_ref, early_ref, kappa_out, norm_out, factor_ref, root_ref, keep_ref, gain_ref, vert_pad,
):
    kappa_out[...] = kappa_ref[...]
    norm_out[...] = norm_ref[...]
    depth, levels = vert_ref.shape[0], factor_ref.shape[0]
    vert_pad[...] = jnp.zeros_like(vert_pad)
    vert_pad[:depth, :depth] = vert_ref[...]
    vert = vert_pad[...]
    head = vert.astype(BF16).astype(F32)
    factor = head + pltpu.roll(head, levels, 1) + pltpu.roll(vert - head, 2 * levels, 1)
    factor_ref[...] = factor.astype(BF16)[:, : 3 * levels]
    planes, height, _ = out_ref.shape
    couple(jnp.sqrt(kappa_ref[...]), tile_rows, root_ref, keep_ref, gain_ref)
    run = columns // WAYS
    groups = LANES // run
    first_row = lax.axis_index("tile") * tile_rows - STEPS
    step_level = wrapped(total_rows * columns * GOLDEN)
    shape = (SUB, LANES)
    group = sum(((iota(shape, 1) >= g * run).astype(I32) for g in range(1, groups)), 0)
    base = (iota(shape, 0) + SUB * group) * step_level
    base = base + (iota(shape, 1) - group * run) * wrapped(WAYS * GOLDEN)
    gain = ROOT12 / 16777216.0
    shift = (0.5 / 16777216.0 - 0.5) * ROOT12
    origin = first_row * wrapped(columns * GOLDEN) + seed_ref[0]
    second = seed_ref[1]

    def one_tile(part, carry):
        start = origin + part * wrapped(groups * SUB * step_level)
        span = pl.ds(pl.multiple_of(part * SUB, SUB), SUB)
        known = {}
        for plane in range(planes):
            offset = start + wrapped(((plane // WAYS) * columns + plane % WAYS) * GOLDEN)
            hashed = mix(mix(base + offset) ^ second)
            drawn = lax.shift_right_logical(hashed, 8).astype(F32)
            drawn = drawn * gain + shift
            row = plane // WAYS - STEPS
            if 0 <= row < tile_rows:
                drawn = drawn * spread(root_ref, plane % WAYS, row)
                known.setdefault((0, row), []).append(drawn)
            out_ref[plane, span, :] = drawn
        for place, (step, row) in enumerate(early_rows(tile_rows)):
            known[step, row] = step_on(
                known[step - 1, row - 1], known[step - 1, row], known[step - 1, row + 1],
                [spread(keep_ref, k, row) for k in range(WAYS)],
                [spread(gain_ref, k, row) for k in range(WAYS)],
                run,
            )
            for k in range(WAYS):
                early_ref[WAYS * place + k, span, :] = known[step, row][k]
        return carry

    lax.fori_loop(0, height // SUB, one_tile, 0)


def field_kernel(
    tiles, noise_ref, early_ref, recv_ref, kappa_ref, norm_ref, factor_ref, prof_hbm, field_ref,
    halo_ref, root_ref, keep_ref, gain_ref, state_ref, hat_ref, prof_ref, sems,
):
    planes, height, _ = noise_ref.shape
    rows = planes // WAYS
    tile_rows, columns = norm_ref.shape
    run = columns // WAYS
    groups = LANES // run
    levels = height * groups
    depth = QUAD * prof_ref.shape[1]
    out_rows = tile_rows + 1
    parts = columns // LANES
    tile = lax.axis_index("tile")

    halo_ref[...] = jnp.zeros_like(halo_ref)
    halo_ref[tile_rows : 2 * tile_rows] = kappa_ref[...]
    for place, shift, count in ((0, -1, tile_rows), (2, 1, tile_rows), (3, 2, 1)):
        source = tile + shift
        valid = ((source >= 0) & (source < tiles)).astype(F32)
        given = recv_ref[place_of(jnp.clip(source, 0, tiles - 1), tiles), : parts * tile_rows, :].astype(F32) * valid
        for k in range(parts):
            halo_ref[place * tile_rows : place * tile_rows + count, k * LANES : (k + 1) * LANES] = (
                given[k * tile_rows : k * tile_rows + count]
            )
    root = jnp.sqrt(halo_ref[...])
    couple(root, rows, root_ref, keep_ref, gain_ref)
    kappa = halo_ref[STEPS : STEPS + out_rows]
    wet = kappa > 0.0
    inverse = jnp.where(wet, root[STEPS : STEPS + out_rows] / jnp.where(wet, kappa, 1.0), 0.0)
    below = recv_ref[place_of(jnp.clip(tile + 1, 0, tiles - 1), tiles), parts * tile_rows :, :].astype(F32)
    norm_below = jnp.concatenate([below[k : k + 1] for k in range(parts)], 1)
    scales = inverse * jnp.concatenate([norm_ref[...], norm_below], 0)

    lower = iota((SUB, LANES), 1) < run

    def diffuse(bundle, carry):
        spans = [
            pl.ds(pl.multiple_of((bundle * TOGETHER + part) * SUB, SUB), SUB) for part in range(TOGETHER)
        ]
        known = [{} for _ in range(STEPS + 1)]

        own = range(STEPS, STEPS + tile_rows)

        def drawn(row):
            cells = [[noise_ref[WAYS * row + k, span, :] for span in spans] for k in range(WAYS)]
            if row not in own:
                scales = [spread(root_ref, k, row) for k in range(WAYS)]
                cells = [[cell * scales[k] for cell in cells[k]] for k in range(WAYS)]
            return cells

        def stepped(step, row):
            if (step, row - STEPS) in early_rows(tile_rows):
                first = WAYS * early_rows(tile_rows).index((step, row - STEPS))
                return [[early_ref[first + k, span, :] for span in spans] for k in range(WAYS)]
            past = known[step - 1]
            keep = [spread(keep_ref, k, row) for k in range(WAYS)]
            gain = [spread(gain_ref, k, row) for k in range(WAYS)]
            fresh = [
                step_on(*([cells[k][part] for k in range(WAYS)] for cells in (
                    past[row - 1], past[row], past[row + 1]
                )), keep, gain, run)
                for part in range(TOGETHER)
            ]
            return [[fresh[part][k] for part in range(TOGETHER)] for k in range(WAYS)]

        for top in range(rows):
            known[0][top] = drawn(top)
            for step in range(1, STEPS + 1):
                row = top - step
                if row < step:
                    break
                known[step][row] = stepped(step, row)
                del known[step - 1][row - 1]
        for row in range(out_rows):
            done = known[STEPS][row + STEPS]
            for k in range(parts):
                for part in range(TOGETHER):
                    one, two = done[2 * k][part], done[2 * k + 1][part]
                    low = jnp.where(lower, one, pltpu.roll(two, run, 1))
                    high = jnp.where(lower, pltpu.roll(one, run, 1), two)
                    state = jnp.concatenate([low, high], 0)
                    head = state.astype(BF16)
                    tail = (state - head.astype(F32)).astype(BF16)
                    first = row * columns + k * LANES
                    for place, piece in enumerate((head, tail, head)):
                        start = place * levels + (bundle * TOGETHER + part) * 2 * SUB
                        at = pl.ds(pl.multiple_of(start, 2 * SUB), 2 * SUB)
                        state_ref[at, first : first + LANES] = piece
        return carry

    lax.fori_loop(0, height // SUB // TOGETHER, diffuse, 0)

    bunch = 2 * SUB
    for row in range(out_rows):
        mixed = jnp.dot(
            factor_ref[...],
            state_ref[:, row * columns : (row + 1) * columns],
            preferred_element_type=F32,
        )
        scaled = (mixed * scales[row : row + 1]).astype(BF16)
        for part in range(levels // bunch):
            first = (part * out_rows + row) * bunch
            field_ref[first : first + bunch, :] = scaled[part * bunch : (part + 1) * bunch]

    col = column_of(iota((columns, 2 * LANES), 0), columns).astype(BF16)

    def positions(pair, first):
        tails = [recv_ref[2 * pair + k, parts * tile_rows :, :].astype(F32) for k in range(2)]
        tail = jnp.concatenate(tails, 1)
        return tail[first : first + 1], tail[first + 1 : first + 2] + tail[first + 2 : first + 3]

    def make_hat(pair, slot):
        near, frac_x = positions(pair, parts)
        hat_ref[slot] = jnp.where(
            col == near.astype(BF16),
            (1.0 - frac_x).astype(BF16),
            jnp.where(col == (near + 1.0).astype(BF16), frac_x.astype(BF16), jnp.zeros_like(col)),
        )

    def answer(pair, hat):
        along = jnp.dot(field_ref[...], hat, preferred_element_type=F32)
        pos_y = sum(positions(pair, parts + 3))
        weights = [jnp.maximum(1.0 - jnp.abs(pos_y - float(row)), 0.0) for row in range(out_rows)]
        for part in range(levels // bunch):
            total = None
            for row in range(out_rows):
                first = (part * out_rows + row) * bunch
                term = along[first : first + bunch] * weights[row]
                total = term if total is None else total + term
            kept = min(bunch // QUAD, -(-(depth - part * bunch) // QUAD))
            at = slice(part * bunch // QUAD, part * bunch // QUAD + kept)
            rounded = total.astype(BF16)[: kept * QUAD]
            for half in range(2):
                lanes = slice(half * LANES, (half + 1) * LANES)
                prof_ref[2 * pair + half, at] = rounded[:, lanes].reshape(kept, QUAD, LANES)

    def some_pairs(step, carry):
        for slot in range(PAIRS):
            make_hat(step * PAIRS + slot, slot)
        for slot in range(PAIRS):
            answer(step * PAIRS + slot, hat_ref[slot])
            if (slot + 1) % SENT == 0:
                sending((step * PAIRS + slot + 1) // SENT - 1).start()
        return carry

    def sending(batch):
        at = pl.ds(batch * 2 * SENT, 2 * SENT)
        return pltpu.make_async_copy(prof_ref.at[at], prof_hbm.at[at], sems.at[batch])

    lax.fori_loop(0, tiles // (2 * PAIRS), some_pairs, 0)
    for batch in range(tiles // (2 * SENT)):
        sending(batch).wait()


def weave_kernel(field_ref, out_ref, flat_ref):
    depth, tile_rows, columns = out_ref.shape
    levels = field_ref.shape[0] // (tile_rows + 1)
    square = (columns, columns)
    weave = (iota(square, 1) == column_of(iota(square, 0), columns)).astype(BF16)
    woven = jnp.dot(field_ref[...], weave, preferred_element_type=F32)
    bunch = 2 * SUB
    for part in range(levels // bunch):
        for row in range(tile_rows):
            first = (part * (tile_rows + 1) + row) * bunch
            flat_ref[part * bunch : (part + 1) * bunch, row, :] = woven[first : first + bunch]
    out_ref[...] = flat_ref[:depth].astype(BF16)


def unpack_kernel(order, given_ref, out_ref, wide_ref, ready_ref, sems):
    depth = out_ref.shape[0]
    bunch = 2 * SUB
    copies = []
    for part, start in enumerate(range(0, depth, bunch)):
        stop = min(start + bunch, depth)
        for place, owner in enumerate(order):
            quads = given_ref[place, start // QUAD : -(-stop // QUAD)]
            rows = quads.reshape(quads.shape[0] * QUAD, LANES)
            wide_ref[start : start + rows.shape[0], owner, :] = rows.astype(F32)
        ready_ref[start:stop] = wide_ref[start:stop].astype(BF16)
        copies.append(
            pltpu.make_async_copy(ready_ref.at[start:stop], out_ref.at[start:stop], sems.at[part])
        )
        copies[-1].start()
    for copy in copies:
        copy.wait()


def body(
    noise_seeds, diffusivity, wet_mask, vert_factor, norm_scale, obs_cell, obs_frac, obs_count
):
    tile_rows, columns = diffusivity.shape
    depth = vert_factor.shape[0]
    levels = up(depth, 2 * SUB)
    tiles = lax.axis_size("tile")
    total_rows = tile_rows * tiles
    groups = LANES * WAYS // columns
    rows = tile_rows + 1 + 2 * STEPS
    slots = obs_cell.shape[2]
    parts = columns // LANES
    square = jax.ShapeDtypeStruct((tile_rows, columns), F32)

    packed, kappa_split, norm_split = pl.pallas_call(
        pack_kernel,
        out_shape=(
            jax.ShapeDtypeStruct((tiles, parts * tile_rows + SUB, LANES), BF16),
            square,
            square,
        ),
        in_specs=[VMEM] * 5 + [SMEM],
        out_specs=(VMEM,) * 3,
        name="pack",
    )(diffusivity, wet_mask, norm_scale, obs_cell[0], obs_frac[0], obs_count)
    order = visiting_order(tiles)
    exchange = dict(
        axis_name="tile", split_axis=0, concat_axis=0, tiled=True, axis_index_groups=[order]
    )
    received = lax.all_to_all(packed, **exchange)

    own = pltpu.VMEM((WAYS, up(tile_rows, SUB), LANES), F32)
    early = len(early_rows(tile_rows))
    noise, ahead, *settled = pl.pallas_call(
        lambda *refs: noise_kernel(total_rows, tile_rows, columns, *refs),
        out_shape=(
            pltpu.VMEM((WAYS * rows, levels // groups, LANES), F32),
            pltpu.VMEM((WAYS * early, levels // groups, LANES), F32),
            pltpu.VMEM(diffusivity.shape, F32),
            pltpu.VMEM(diffusivity.shape, F32),
            pltpu.VMEM((levels, 3 * levels), BF16),
        ),
        in_specs=[SMEM, VMEM, VMEM, VMEM],
        out_specs=(VMEM,) * 5,
        scratch_shapes=[own, own, own, pltpu.VMEM((levels, up(3 * levels, LANES)), F32)],
        name="noise",
        compiler_params=LIMIT,
    )(*(distant(part) for part in (noise_seeds, kappa_split, norm_split, vert_factor)))

    coefficients = pltpu.VMEM((WAYS, up(rows, SUB), LANES), F32)
    answers, field = pl.pallas_call(
        lambda *refs: field_kernel(tiles, *refs),
        out_shape=(
            pltpu.HBM((tiles, up(depth, QUAD) // QUAD, QUAD, slots), BF16),
            pltpu.VMEM(((tile_rows + 1) * levels, columns), BF16),
        ),
        in_specs=[VMEM] * 6,
        out_specs=(ANY, VMEM),
        scratch_shapes=[
            pltpu.VMEM((up(rows, SUB), columns), F32),
            coefficients,
            coefficients,
            coefficients,
            pltpu.VMEM((3 * levels, (tile_rows + 1) * columns), BF16),
            pltpu.VMEM((PAIRS, columns, 2 * LANES), BF16),
            pltpu.VMEM((tiles, up(depth, QUAD) // QUAD, QUAD, slots), BF16),
            pltpu.SemaphoreType.DMA((tiles // (2 * SENT),)),
        ],
        name="field",
        compiler_params=LIMIT,
    )(
        *(resident(part) for part in (noise, ahead, received, *settled))
    )
    gathered = lax.all_to_all(answers, **exchange)
    perturbation = pl.pallas_call(
        weave_kernel,
        out_shape=jax.ShapeDtypeStruct((depth, tile_rows, columns), BF16),
        in_specs=[VMEM],
        out_specs=VMEM,
        scratch_shapes=[pltpu.VMEM((levels, tile_rows, columns), F32)],
        name="weave",
        compiler_params=LIMIT,
    )(resident(field))
    chunks = levels // (2 * SUB)
    profiles = pl.pallas_call(
        lambda *refs: unpack_kernel(order, *refs),
        out_shape=jax.ShapeDtypeStruct((depth, tiles, slots), BF16),
        in_specs=[VMEM],
        out_specs=ANY,
        scratch_shapes=[
            pltpu.VMEM((levels, tiles, slots), F32),
            pltpu.VMEM((levels, tiles, slots), BF16),
            pltpu.SemaphoreType.DMA((chunks,)),
        ],
        name="unpack",
        compiler_params=LIMIT,
    )(resident(gathered))
    return (perturbation, jnp.transpose(profiles, (1, 0, 2))[None])


def solution(mesh):
    in_specs = (
        P("member"),
        P("tile", None),
        P("tile", None),
        P(),
        P("tile", None),
        P("tile", None, None),
        P("tile", None, None, None),
        P("tile", None),
    )
    out_specs = (P("member", "tile", None), P("tile", None, "member", None))
    return jax.shard_map(body, mesh=mesh, in_specs=in_specs, out_specs=out_specs, check_vma=False)
```

```python
import jax
import jax.numpy as jnp
from jax import lax
from jax.experimental import pallas as pl
from jax.experimental.pallas import tpu as pltpu
from jax.sharding import PartitionSpec as P

STEPS = 8
LANES = 128
SUB = 8
EXACT = lax.Precision.HIGHEST
F32 = jnp.float32
BF16 = jnp.bfloat16
WAYS = 4
TOGETHER = 5
PAIRS = 8
SENT = 2
QUAD = 4
I32 = jnp.int32
GOLDEN = -1640531535
ROOT12 = 3.4641016151377544
VMEM = pl.BlockSpec(memory_space=pltpu.VMEM)
SMEM = pl.BlockSpec(memory_space=pltpu.SMEM)
ANY = pl.BlockSpec(memory_space=pl.ANY)
LIMIT = pltpu.CompilerParams(vmem_limit_bytes=24 << 20)


def resident(array):
    return pltpu.with_memory_space_constraint(array, pltpu.VMEM)


def distant(array):
    return pltpu.with_memory_space_constraint(array, pltpu.HBM)


def up(value, unit):
    return -(-value // unit) * unit


def wrapped(value):
    return (value + 2**31) % 2**32 - 2**31


def iota(shape, axis):
    return lax.broadcasted_iota(I32, shape, axis)


def visiting_order(tiles):
    pairs = tiles // 2
    ring = list(range(1, pairs, 2)) + list(range(0, pairs, 2))[::-1]
    turn = pairs // 4
    return [2 * pair + core for pair in ring[turn:] + ring[:turn] for core in (1, 0)]


def place_of(tile, tiles):
    order = visiting_order(tiles)
    return sum(jnp.where(tile == order[place], place, 0) for place in range(1, tiles))


def column_of(place, columns):
    run = columns // WAYS
    turn = sum(((place >= k * run).astype(I32) for k in range(1, WAYS)), jnp.zeros_like(place))
    return WAYS * (place - turn * run) + turn


def pack_kernel(
    diff_ref, wet_ref, norm_ref, cell_ref, frac_ref, count_ref, out_ref, kappa_out, norm_out
):
    tile_rows, columns = diff_ref.shape
    owners = cell_ref.shape[0]
    order = visiting_order(owners)
    kappa = diff_ref[...] * wet_ref[...].astype(F32)
    square = (columns, columns)
    parting = (iota(square, 0) == column_of(iota((1, columns), 1), columns)).astype(F32)
    both = jnp.concatenate([kappa, norm_ref[...]], 0)
    parted = jnp.dot(both, parting, precision=EXACT, preferred_element_type=F32)
    kappa_out[...] = parted[:tile_rows]
    norm_out[...] = parted[tile_rows:]
    parts = columns // LANES
    halo = jnp.concatenate(
        [parted[:tile_rows, k * LANES : (k + 1) * LANES] for k in range(parts)], 0
    ).astype(BF16)
    norms = [parted[tile_rows : tile_rows + 1, k * LANES : (k + 1) * LANES] for k in range(parts)]
    cell = cell_ref[...]
    row = jnp.zeros_like(cell)
    for step in range(1, tile_rows):
        row = row + (cell >= step * columns).astype(I32)
    col = (cell - row * columns).astype(F32)
    row = row.astype(F32)
    frac_y, frac_x = frac_ref[:, 0, :], frac_ref[:, 1, :]
    high_y, high_x = (frac.astype(BF16).astype(F32) for frac in (frac_y, frac_x))
    low_y, low_x = frac_y - high_y, frac_x - high_x
    lane = iota((1, LANES), 1)
    for owner in range(owners):
        at = slice(owner, owner + 1)
        live = lane < count_ref[0, owner]
        tail = jnp.concatenate(
            norms + [col[at], high_x[at], low_x[at]]
            + [jnp.where(live, row[at], -16.0), high_y[at], low_y[at]],
            0,
        )
        at = order.index(owner)
        out_ref[at, : parts * tile_rows, :] = halo
        out_ref[at, parts * tile_rows :, :] = tail.astype(BF16)


def mix(hashed):
    hashed = (hashed ^ lax.shift_right_logical(hashed, 16)) * -2048144789
    hashed = (hashed ^ lax.shift_right_logical(hashed, 13)) * -1028477387
    hashed = hashed ^ lax.shift_right_logical(hashed, 16)
    return hashed


def spread(ref, k, row):
    return ref[k, pl.ds(row, SUB, stride=0), :]


def couple(root, rows, root_ref, keep_ref, gain_ref):
    run = root.shape[1] // WAYS
    groups = LANES // run
    lane = iota((1, LANES), 1)
    roots = []
    for k in range(WAYS):
        vector = root[:, (k // groups) * LANES : (k // groups + 1) * LANES]
        turned = pltpu.roll(vector, run, 1)
        keeps = (lane >= run) if k % groups else (lane < run)
        roots.append(jnp.where(keeps, vector, turned))
        root_ref[k, : root.shape[0]] = roots[k]
    low, high = (lane == 0) | (lane == run), (lane == run - 1) | (lane == LANES - 1)
    inner = slice(1, rows - 1)
    west = [jnp.where(low, 0.0, pltpu.roll(roots[-1], 1, 1))] + roots[:-1]
    east = roots[1:] + [jnp.where(high, 0.0, pltpu.roll(roots[0], LANES - 1, 1))]
    for k in range(WAYS):
        near = root_ref[k, : rows - 2] + root_ref[k, 2:rows] + (west[k] + east[k])[inner]
        keep_ref[k, inner] = 1.0 - roots[k][inner] * near
        gain_ref[k, inner] = roots[k][inner] * roots[k][inner]


def step_on(above, here, under, keep, gain, run):
    lanes = iota((SUB, LANES), 1)
    low, high = (lanes == 0) | (lanes == run), (lanes == run - 1) | (lanes == LANES - 1)
    west = [jnp.where(low, 0.0, pltpu.roll(here[-1], 1, 1))] + here[:-1]
    east = here[1:] + [jnp.where(high, 0.0, pltpu.roll(here[0], LANES - 1, 1))]
    return [
        keep[k] * here[k] + gain[k] * ((above[k] + under[k]) + (west[k] + east[k]))
        for k in range(WAYS)
    ]


def early_rows(tile_rows):
    steps = range(1, min(STEPS, (tile_rows - 1) // 2) + 1)
    return [(step, row) for step in steps for row in range(step, tile_rows - step)]


def noise_kernel(
    total_rows, tile_rows, columns, seed_ref, kappa_ref, norm_ref, vert_ref,
    out_ref, early_ref, kappa_out, norm_out, factor_ref, root_ref, keep_ref, gain_ref, vert_pad,
):
    kappa_out[...] = kappa_ref[...]
    norm_out[...] = norm_ref[...]
    depth, levels = vert_ref.shape[0], factor_ref.shape[0]
    vert_pad[...] = jnp.zeros_like(vert_pad)
    vert_pad[:depth, :depth] = vert_ref[...]
    vert = vert_pad[...]
    head = vert.astype(BF16).astype(F32)
    factor = head + pltpu.roll(head, levels, 1) + pltpu.roll(vert - head, 2 * levels, 1)
    factor_ref[...] = factor.astype(BF16)[:, : 3 * levels]
    planes, height, _ = out_ref.shape
    couple(jnp.sqrt(kappa_ref[...]), tile_rows, root_ref, keep_ref, gain_ref)
    run = columns // WAYS
    groups = LANES // run
    first_row = lax.axis_index("tile") * tile_rows - STEPS
    step_level = wrapped(total_rows * columns * GOLDEN)
    shape = (SUB, LANES)
    group = sum(((iota(shape, 1) >= g * run).astype(I32) for g in range(1, groups)), 0)
    base = (iota(shape, 0) + SUB * group) * step_level
    base = base + (iota(shape, 1) - group * run) * wrapped(WAYS * GOLDEN)
    gain = ROOT12 / 16777216.0
    shift = (0.5 / 16777216.0 - 0.5) * ROOT12
    origin = first_row * wrapped(columns * GOLDEN) + seed_ref[0]
    second = seed_ref[1]

    def one_tile(part, carry):
        start = origin + part * wrapped(groups * SUB * step_level)
        span = pl.ds(pl.multiple_of(part * SUB, SUB), SUB)
        known = {}
        for plane in range(planes):
            offset = start + wrapped(((plane // WAYS) * columns + plane % WAYS) * GOLDEN)
            hashed = mix(mix(base + offset) ^ second)
            drawn = lax.shift_right_logical(hashed, 8).astype(F32)
            drawn = drawn * gain + shift
            row = plane // WAYS - STEPS
            if 0 <= row < tile_rows:
                drawn = drawn * spread(root_ref, plane % WAYS, row)
                known.setdefault((0, row), []).append(drawn)
            out_ref[plane, span, :] = drawn
        for place, (step, row) in enumerate(early_rows(tile_rows)):
            known[step, row] = step_on(
                known[step - 1, row - 1], known[step - 1, row], known[step - 1, row + 1],
                [spread(keep_ref, k, row) for k in range(WAYS)],
                [spread(gain_ref, k, row) for k in range(WAYS)],
                run,
            )
            for k in range(WAYS):
                early_ref[WAYS * place + k, span, :] = known[step, row][k]
        return carry

    lax.fori_loop(0, height // SUB, one_tile, 0)


def field_kernel(
    tiles, noise_ref, early_ref, recv_ref, kappa_ref, norm_ref, factor_ref, prof_hbm, field_ref,
    halo_ref, root_ref, keep_ref, gain_ref, state_ref, hat_ref, prof_ref, sems,
):
    planes, height, _ = noise_ref.shape
    rows = planes // WAYS
    tile_rows, columns = norm_ref.shape
    run = columns // WAYS
    groups = LANES // run
    levels = height * groups
    depth = QUAD * prof_ref.shape[1]
    out_rows = tile_rows + 1
    parts = columns // LANES
    tile = lax.axis_index("tile")

    halo_ref[...] = jnp.zeros_like(halo_ref)
    halo_ref[tile_rows : 2 * tile_rows] = kappa_ref[...]
    for place, shift, count in ((0, -1, tile_rows), (2, 1, tile_rows), (3, 2, 1)):
        source = tile + shift
        valid = ((source >= 0) & (source < tiles)).astype(F32)
        given = recv_ref[place_of(jnp.clip(source, 0, tiles - 1), tiles), : parts * tile_rows, :].astype(F32) * valid
        for k in range(parts):
            halo_ref[place * tile_rows : place * tile_rows + count, k * LANES : (k + 1) * LANES] = (
                given[k * tile_rows : k * tile_rows + count]
            )
    root = jnp.sqrt(halo_ref[...])
    couple(root, rows, root_ref, keep_ref, gain_ref)
    kappa = halo_ref[STEPS : STEPS + out_rows]
    wet = kappa > 0.0
    inverse = jnp.where(wet, root[STEPS : STEPS + out_rows] / jnp.where(wet, kappa, 1.0), 0.0)
    below = recv_ref[place_of(jnp.clip(tile + 1, 0, tiles - 1), tiles), parts * tile_rows :, :].astype(F32)
    norm_below = jnp.concatenate([below[k : k + 1] for k in range(parts)], 1)
    scales = inverse * jnp.concatenate([norm_ref[...], norm_below], 0)

    lower = iota((SUB, LANES), 1) < run

    def diffuse(bundle, carry):
        spans = [
            pl.ds(pl.multiple_of((bundle * TOGETHER + part) * SUB, SUB), SUB) for part in range(TOGETHER)
        ]
        known = [{} for _ in range(STEPS + 1)]

        own = range(STEPS, STEPS + tile_rows)

        def drawn(row):
            cells = [[noise_ref[WAYS * row + k, span, :] for span in spans] for k in range(WAYS)]
            if row not in own:
                scales = [spread(root_ref, k, row) for k in range(WAYS)]
                cells = [[cell * scales[k] for cell in cells[k]] for k in range(WAYS)]
            return cells

        def stepped(step, row):
            if (step, row - STEPS) in early_rows(tile_rows):
                first = WAYS * early_rows(tile_rows).index((step, row - STEPS))
                return [[early_ref[first + k, span, :] for span in spans] for k in range(WAYS)]
            past = known[step - 1]
            keep = [spread(keep_ref, k, row) for k in range(WAYS)]
            gain = [spread(gain_ref, k, row) for k in range(WAYS)]
            fresh = [
                step_on(*([cells[k][part] for k in range(WAYS)] for cells in (
                    past[row - 1], past[row], past[row + 1]
                )), keep, gain, run)
                for part in range(TOGETHER)
            ]
            return [[fresh[part][k] for part in range(TOGETHER)] for k in range(WAYS)]

        for top in range(rows):
            known[0][top] = drawn(top)
            for step in range(1, STEPS + 1):
                row = top - step
                if row < step:
                    break
                known[step][row] = stepped(step, row)
                del known[step - 1][row - 1]
        for row in range(out_rows):
            done = known[STEPS][row + STEPS]
            for k in range(parts):
                for part in range(TOGETHER):
                    one, two = done[2 * k][part], done[2 * k + 1][part]
                    low = jnp.where(lower, one, pltpu.roll(two, run, 1))
                    high = jnp.where(lower, pltpu.roll(one, run, 1), two)
                    state = jnp.concatenate([low, high], 0)
                    head = state.astype(BF16)
                    tail = (state - head.astype(F32)).astype(BF16)
                    first = row * columns + k * LANES
                    for place, piece in enumerate((head, tail, head)):
                        start = place * levels + (bundle * TOGETHER + part) * 2 * SUB
                        at = pl.ds(pl.multiple_of(start, 2 * SUB), 2 * SUB)
                        state_ref[at, first : first + LANES] = piece
        return carry

    lax.fori_loop(0, height // SUB // TOGETHER, diffuse, 0)

    bunch = 2 * SUB
    for row in range(out_rows):
        mixed = jnp.dot(
            factor_ref[...],
            state_ref[:, row * columns : (row + 1) * columns],
            preferred_element_type=F32,
        )
        scaled = (mixed * scales[row : row + 1]).astype(BF16)
        for part in range(levels // bunch):
            first = (part * out_rows + row) * bunch
            field_ref[first : first + bunch, :] = scaled[part * bunch : (part + 1) * bunch]

    col = column_of(iota((columns, 2 * LANES), 0), columns).astype(BF16)

    def positions(pair, first):
        tails = [recv_ref[2 * pair + k, parts * tile_rows :, :].astype(F32) for k in range(2)]
        tail = jnp.concatenate(tails, 1)
        return tail[first : first + 1], tail[first + 1 : first + 2] + tail[first + 2 : first + 3]

    def make_hat(pair, slot):
        near, frac_x = positions(pair, parts)
        hat_ref[slot] = jnp.where(
            col == near.astype(BF16),
            (1.0 - frac_x).astype(BF16),
            jnp.where(col == (near + 1.0).astype(BF16), frac_x.astype(BF16), jnp.zeros_like(col)),
        )

    def answer(pair, hat):
        along = jnp.dot(field_ref[...], hat, preferred_element_type=F32)
        pos_y = sum(positions(pair, parts + 3))
        weights = [jnp.maximum(1.0 - jnp.abs(pos_y - float(row)), 0.0) for row in range(out_rows)]
        for part in range(levels // bunch):
            terms = []
            for row in range(out_rows):
                first = (part * out_rows + row) * bunch
                terms.append(along[first : first + bunch] * weights[row])
            while len(terms) > 1:
                paired = [one + two for one, two in zip(terms[::2], terms[1::2])]
                terms = paired + terms[2 * len(paired) :]
            total = terms[0]
            kept = min(bunch // QUAD, -(-(depth - part * bunch) // QUAD))
            at = slice(part * bunch // QUAD, part * bunch // QUAD + kept)
            rounded = total.astype(BF16)[: kept * QUAD]
            for half in range(2):
                lanes = slice(half * LANES, (half + 1) * LANES)
                prof_ref[2 * pair + half, at] = rounded[:, lanes].reshape(kept, QUAD, LANES)

    def some_pairs(step, carry):
        for slot in range(PAIRS):
            make_hat(step * PAIRS + slot, slot)
        for slot in range(PAIRS):
            answer(step * PAIRS + slot, hat_ref[slot])
            if (slot + 1) % SENT == 0:
                sending((step * PAIRS + slot + 1) // SENT - 1).start()
        return carry

    def sending(batch):
        at = pl.ds(batch * 2 * SENT, 2 * SENT)
        return pltpu.make_async_copy(prof_ref.at[at], prof_hbm.at[at], sems.at[batch])

    lax.fori_loop(0, tiles // (2 * PAIRS), some_pairs, 0)
    for batch in range(tiles // (2 * SENT)):
        sending(batch).wait()


def weave_kernel(field_ref, out_ref, flat_ref):
    depth, tile_rows, columns = out_ref.shape
    levels = field_ref.shape[0] // (tile_rows + 1)
    square = (columns, columns)
    weave = (iota(square, 1) == column_of(iota(square, 0), columns)).astype(BF16)
    woven = jnp.dot(field_ref[...], weave, preferred_element_type=F32)
    bunch = 2 * SUB
    for part in range(levels // bunch):
        for row in range(tile_rows):
            first = (part * (tile_rows + 1) + row) * bunch
            flat_ref[part * bunch : (part + 1) * bunch, row, :] = woven[first : first + bunch]
    out_ref[...] = flat_ref[:depth].astype(BF16)


def unpack_kernel(order, given_ref, out_ref, wide_ref, ready_ref, sems):
    depth = out_ref.shape[0]
    bunch = 2 * SUB
    copies = []
    for part, start in enumerate(range(0, depth, bunch)):
        stop = min(start + bunch, depth)
        for place, owner in enumerate(order):
            quads = given_ref[place, start // QUAD : -(-stop // QUAD)]
            rows = quads.reshape(quads.shape[0] * QUAD, LANES)
            wide_ref[start : start + rows.shape[0], owner, :] = rows.astype(F32)
        ready_ref[start:stop] = wide_ref[start:stop].astype(BF16)
        copies.append(
            pltpu.make_async_copy(ready_ref.at[start:stop], out_ref.at[start:stop], sems.at[part])
        )
        copies[-1].start()
    for copy in copies:
        copy.wait()


def body(
    noise_seeds, diffusivity, wet_mask, vert_factor, norm_scale, obs_cell, obs_frac, obs_count
):
    tile_rows, columns = diffusivity.shape
    depth = vert_factor.shape[0]
    levels = up(depth, 2 * SUB)
    tiles = lax.axis_size("tile")
    total_rows = tile_rows * tiles
    groups = LANES * WAYS // columns
    rows = tile_rows + 1 + 2 * STEPS
    slots = obs_cell.shape[2]
    parts = columns // LANES
    square = jax.ShapeDtypeStruct((tile_rows, columns), F32)

    packed, kappa_split, norm_split = pl.pallas_call(
        pack_kernel,
        out_shape=(
            jax.ShapeDtypeStruct((tiles, parts * tile_rows + SUB, LANES), BF16),
            square,
            square,
        ),
        in_specs=[VMEM] * 5 + [SMEM],
        out_specs=(VMEM,) * 3,
        name="pack",
    )(diffusivity, wet_mask, norm_scale, obs_cell[0], obs_frac[0], obs_count)
    order = visiting_order(tiles)
    exchange = dict(
        axis_name="tile", split_axis=0, concat_axis=0, tiled=True, axis_index_groups=[order]
    )
    received = lax.all_to_all(packed, **exchange)

    own = pltpu.VMEM((WAYS, up(tile_rows, SUB) + SUB, LANES), F32)
    early = len(early_rows(tile_rows))
    noise, ahead, *settled = pl.pallas_call(
        lambda *refs: noise_kernel(total_rows, tile_rows, columns, *refs),
        out_shape=(
            pltpu.VMEM((WAYS * rows, levels // groups, LANES), F32),
            pltpu.VMEM((WAYS * early, levels // groups, LANES), F32),
            pltpu.VMEM(diffusivity.shape, F32),
            pltpu.VMEM(diffusivity.shape, F32),
            pltpu.VMEM((levels, 3 * levels), BF16),
        ),
        in_specs=[SMEM, VMEM, VMEM, VMEM],
        out_specs=(VMEM,) * 5,
        scratch_shapes=[own, own, own, pltpu.VMEM((levels, up(3 * levels, LANES)), F32)],
        name="noise",
        compiler_params=LIMIT,
    )(*(distant(part) for part in (noise_seeds, kappa_split, norm_split, vert_factor)))

    coefficients = pltpu.VMEM((WAYS, up(rows, SUB), LANES), F32)
    answers, field = pl.pallas_call(
        lambda *refs: field_kernel(tiles, *refs),
        out_shape=(
            pltpu.HBM((tiles, up(depth, QUAD) // QUAD, QUAD, slots), BF16),
            pltpu.VMEM(((tile_rows + 1) * levels, columns), BF16),
        ),
        in_specs=[VMEM] * 6,
        out_specs=(ANY, VMEM),
        scratch_shapes=[
            pltpu.VMEM((up(rows, SUB), columns), F32),
            coefficients,
            coefficients,
            coefficients,
            pltpu.VMEM((3 * levels, (tile_rows + 1) * columns), BF16),
            pltpu.VMEM((PAIRS, columns, 2 * LANES), BF16),
            pltpu.VMEM((tiles, up(depth, QUAD) // QUAD, QUAD, slots), BF16),
            pltpu.SemaphoreType.DMA((tiles // (2 * SENT),)),
        ],
        name="field",
        compiler_params=LIMIT,
    )(
        *(resident(part) for part in (noise, ahead, received, *settled))
    )
    gathered = lax.all_to_all(answers, **exchange)
    perturbation = pl.pallas_call(
        weave_kernel,
        out_shape=jax.ShapeDtypeStruct((depth, tile_rows, columns), BF16),
        in_specs=[VMEM],
        out_specs=VMEM,
        scratch_shapes=[pltpu.VMEM((levels, tile_rows, columns), F32)],
        name="weave",
        compiler_params=LIMIT,
    )(resident(field))
    chunks = levels // (2 * SUB)
    profiles = pl.pallas_call(
        lambda *refs: unpack_kernel(order, *refs),
        out_shape=jax.ShapeDtypeStruct((depth, tiles, slots), BF16),
        in_specs=[VMEM],
        out_specs=ANY,
        scratch_shapes=[
            pltpu.VMEM((levels, tiles, slots), F32),
            pltpu.VMEM((levels, tiles, slots), BF16),
            pltpu.SemaphoreType.DMA((chunks,)),
        ],
        name="unpack",
        compiler_params=LIMIT,
    )(resident(gathered))
    return (perturbation, jnp.transpose(profiles, (1, 0, 2))[None])


def solution(mesh):
    in_specs = (
        P("member"),
        P("tile", None),
        P("tile", None),
        P(),
        P("tile", None),
        P("tile", None, None),
        P("tile", None, None, None),
        P("tile", None),
    )
    out_specs = (P("member", "tile", None), P("tile", None, "member", None))
    return jax.shard_map(body, mesh=mesh, in_specs=in_specs, out_specs=out_specs, check_vma=False)
```

```python
import jax
import jax.numpy as jnp
from jax import lax
from jax.experimental import pallas as pl
from jax.experimental.pallas import tpu as pltpu
from jax.sharding import PartitionSpec as P

STEPS = 8
LANES = 128
SUB = 8
EXACT = lax.Precision.HIGHEST
F32 = jnp.float32
BF16 = jnp.bfloat16
WAYS = 4
TOGETHER = 5
PAIRS = 8
SENT = 2
QUAD = 4
I32 = jnp.int32
GOLDEN = -1640531535
ROOT12 = 3.4641016151377544
VMEM = pl.BlockSpec(memory_space=pltpu.VMEM)
SMEM = pl.BlockSpec(memory_space=pltpu.SMEM)
ANY = pl.BlockSpec(memory_space=pl.ANY)
LIMIT = pltpu.CompilerParams(vmem_limit_bytes=24 << 20)


def resident(array):
    return pltpu.with_memory_space_constraint(array, pltpu.VMEM)


def distant(array):
    return pltpu.with_memory_space_constraint(array, pltpu.HBM)


def up(value, unit):
    return -(-value // unit) * unit


def wrapped(value):
    return (value + 2**31) % 2**32 - 2**31


def iota(shape, axis):
    return lax.broadcasted_iota(I32, shape, axis)


def visiting_order(tiles):
    pairs = tiles // 2
    ring = list(range(1, pairs, 2)) + list(range(0, pairs, 2))[::-1]
    turn = pairs // 4
    return [2 * pair + core for pair in ring[turn:] + ring[:turn] for core in (1, 0)]


def place_of(tile, tiles):
    order = visiting_order(tiles)
    return sum(jnp.where(tile == order[place], place, 0) for place in range(1, tiles))


def column_of(place, columns):
    run = columns // WAYS
    turn = sum(((place >= k * run).astype(I32) for k in range(1, WAYS)), jnp.zeros_like(place))
    return WAYS * (place - turn * run) + turn


def pack_kernel(
    diff_ref, wet_ref, norm_ref, cell_ref, frac_ref, count_ref, out_ref, kappa_out, norm_out
):
    tile_rows, columns = diff_ref.shape
    owners = cell_ref.shape[0]
    order = visiting_order(owners)
    kappa = diff_ref[...] * wet_ref[...].astype(F32)
    square = (columns, columns)
    parting = (iota(square, 0) == column_of(iota((1, columns), 1), columns)).astype(F32)
    both = jnp.concatenate([kappa, norm_ref[...]], 0)
    parted = jnp.dot(both, parting, precision=EXACT, preferred_element_type=F32)
    kappa_out[...] = parted[:tile_rows]
    norm_out[...] = parted[tile_rows:]
    parts = columns // LANES
    halo = jnp.concatenate(
        [parted[:tile_rows, k * LANES : (k + 1) * LANES] for k in range(parts)], 0
    ).astype(BF16)
    norms = [parted[tile_rows : tile_rows + 1, k * LANES : (k + 1) * LANES] for k in range(parts)]
    cell = cell_ref[...]
    row = jnp.zeros_like(cell)
    for step in range(1, tile_rows):
        row = row + (cell >= step * columns).astype(I32)
    col = (cell - row * columns).astype(F32)
    row = row.astype(F32)
    frac_y, frac_x = frac_ref[:, 0, :], frac_ref[:, 1, :]
    high_y, high_x = (frac.astype(BF16).astype(F32) for frac in (frac_y, frac_x))
    low_y, low_x = frac_y - high_y, frac_x - high_x
    lane = iota((1, LANES), 1)
    for owner in range(owners):
        at = slice(owner, owner + 1)
        live = lane < count_ref[0, owner]
        tail = jnp.concatenate(
            norms + [col[at], high_x[at], low_x[at]]
            + [jnp.where(live, row[at], -16.0), high_y[at], low_y[at]],
            0,
        )
        at = order.index(owner)
        out_ref[at, : parts * tile_rows, :] = halo
        out_ref[at, parts * tile_rows :, :] = tail.astype(BF16)


def mix(hashed):
    hashed = (hashed ^ lax.shift_right_logical(hashed, 16)) * -2048144789
    hashed = (hashed ^ lax.shift_right_logical(hashed, 13)) * -1028477387
    hashed = hashed ^ lax.shift_right_logical(hashed, 16)
    return hashed


def spread(ref, k, row):
    return ref[k, pl.ds(row, SUB, stride=0), :]


def couple(root, rows, root_ref, keep_ref, gain_ref):
    run = root.shape[1] // WAYS
    groups = LANES // run
    lane = iota((1, LANES), 1)
    roots = []
    for k in range(WAYS):
        vector = root[:, (k // groups) * LANES : (k // groups + 1) * LANES]
        turned = pltpu.roll(vector, run, 1)
        keeps = (lane >= run) if k % groups else (lane < run)
        roots.append(jnp.where(keeps, vector, turned))
        root_ref[k, : root.shape[0]] = roots[k]
    low, high = (lane == 0) | (lane == run), (lane == run - 1) | (lane == LANES - 1)
    inner = slice(1, rows - 1)
    west = [jnp.where(low, 0.0, pltpu.roll(roots[-1], 1, 1))] + roots[:-1]
    east = roots[1:] + [jnp.where(high, 0.0, pltpu.roll(roots[0], LANES - 1, 1))]
    for k in range(WAYS):
        near = root_ref[k, : rows - 2] + root_ref[k, 2:rows] + (west[k] + east[k])[inner]
        keep_ref[k, inner] = 1.0 - roots[k][inner] * near
        gain_ref[k, inner] = roots[k][inner] * roots[k][inner]


def step_on(above, here, under, keep, gain, run):
    lanes = iota((SUB, LANES), 1)
    low, high = (lanes == 0) | (lanes == run), (lanes == run - 1) | (lanes == LANES - 1)
    west = [jnp.where(low, 0.0, pltpu.roll(here[-1], 1, 1))] + here[:-1]
    east = here[1:] + [jnp.where(high, 0.0, pltpu.roll(here[0], LANES - 1, 1))]
    return [
        keep[k] * here[k] + gain[k] * ((above[k] + under[k]) + (west[k] + east[k]))
        for k in range(WAYS)
    ]


def early_rows(tile_rows):
    steps = range(1, min(STEPS, (tile_rows - 1) // 2) + 1)
    return [(step, row) for step in steps for row in range(step, tile_rows - step)]


def noise_kernel(
    total_rows, tile_rows, columns, seed_ref, kappa_ref, norm_ref, vert_ref,
    out_ref, early_ref, kappa_out, norm_out, factor_ref, root_ref, keep_ref, gain_ref, vert_pad,
):
    kappa_out[...] = kappa_ref[...]
    norm_out[...] = norm_ref[...]
    depth, levels = vert_ref.shape[0], factor_ref.shape[0]
    vert_pad[...] = jnp.zeros_like(vert_pad)
    vert_pad[:depth, :depth] = vert_ref[...]
    vert = vert_pad[...]
    head = vert.astype(BF16).astype(F32)
    factor = head + pltpu.roll(head, levels, 1) + pltpu.roll(vert - head, 2 * levels, 1)
    factor_ref[...] = factor.astype(BF16)[:, : 3 * levels]
    planes, height, _ = out_ref.shape
    couple(jnp.sqrt(kappa_ref[...]), tile_rows, root_ref, keep_ref, gain_ref)
    run = columns // WAYS
    groups = LANES // run
    first_row = lax.axis_index("tile") * tile_rows - STEPS
    step_level = wrapped(total_rows * columns * GOLDEN)
    shape = (SUB, LANES)
    group = sum(((iota(shape, 1) >= g * run).astype(I32) for g in range(1, groups)), 0)
    base = (iota(shape, 0) + SUB * group) * step_level
    base = base + (iota(shape, 1) - group * run) * wrapped(WAYS * GOLDEN)
    gain = ROOT12 / 16777216.0
    shift = (0.5 / 16777216.0 - 0.5) * ROOT12
    origin = first_row * wrapped(columns * GOLDEN) + seed_ref[0]
    second = seed_ref[1]

    def one_tile(part, carry):
        start = origin + part * wrapped(groups * SUB * step_level)
        span = pl.ds(pl.multiple_of(part * SUB, SUB), SUB)
        known = {}
        for plane in range(planes):
            offset = start + wrapped(((plane // WAYS) * columns + plane % WAYS) * GOLDEN)
            hashed = mix(mix(base + offset) ^ second)
            drawn = lax.shift_right_logical(hashed, 8).astype(F32)
            drawn = drawn * gain + shift
            row = plane // WAYS - STEPS
            if 0 <= row < tile_rows:
                drawn = drawn * spread(root_ref, plane % WAYS, row)
                known.setdefault((0, row), []).append(drawn)
            out_ref[plane, span, :] = drawn
        for place, (step, row) in enumerate(early_rows(tile_rows)):
            known[step, row] = step_on(
                known[step - 1, row - 1], known[step - 1, row], known[step - 1, row + 1],
                [spread(keep_ref, k, row) for k in range(WAYS)],
                [spread(gain_ref, k, row) for k in range(WAYS)],
                run,
            )
            for k in range(WAYS):
                early_ref[WAYS * place + k, span, :] = known[step, row][k]
        return carry

    lax.fori_loop(0, height // SUB, one_tile, 0)


def field_kernel(
    tiles, noise_ref, early_ref, recv_ref, kappa_ref, norm_ref, factor_ref, prof_hbm, field_ref,
    halo_ref, root_ref, keep_ref, gain_ref, state_ref, hat_ref, prof_ref, sems,
):
    planes, height, _ = noise_ref.shape
    rows = planes // WAYS
    tile_rows, columns = norm_ref.shape
    run = columns // WAYS
    groups = LANES // run
    levels = height * groups
    depth = QUAD * prof_ref.shape[1]
    out_rows = tile_rows + 1
    parts = columns // LANES
    tile = lax.axis_index("tile")

    halo_ref[...] = jnp.zeros_like(halo_ref)
    halo_ref[tile_rows : 2 * tile_rows] = kappa_ref[...]
    for place, shift, count in ((0, -1, tile_rows), (2, 1, tile_rows), (3, 2, 1)):
        source = tile + shift
        valid = ((source >= 0) & (source < tiles)).astype(F32)
        given = recv_ref[place_of(jnp.clip(source, 0, tiles - 1), tiles), : parts * tile_rows, :].astype(F32) * valid
        for k in range(parts):
            halo_ref[place * tile_rows : place * tile_rows + count, k * LANES : (k + 1) * LANES] = (
                given[k * tile_rows : k * tile_rows + count]
            )
    root = jnp.sqrt(halo_ref[...])
    couple(root, rows, root_ref, keep_ref, gain_ref)
    kappa = halo_ref[STEPS : STEPS + out_rows]
    wet = kappa > 0.0
    inverse = jnp.where(wet, root[STEPS : STEPS + out_rows] / jnp.where(wet, kappa, 1.0), 0.0)
    below = recv_ref[place_of(jnp.clip(tile + 1, 0, tiles - 1), tiles), parts * tile_rows :, :].astype(F32)
    norm_below = jnp.concatenate([below[k : k + 1] for k in range(parts)], 1)
    scales = inverse * jnp.concatenate([norm_ref[...], norm_below], 0)

    lower = iota((SUB, LANES), 1) < run

    def diffuse(bundle, carry):
        spans = [
            pl.ds(pl.multiple_of((bundle * TOGETHER + part) * SUB, SUB), SUB) for part in range(TOGETHER)
        ]
        known = [{} for _ in range(STEPS + 1)]

        own = range(STEPS, STEPS + tile_rows)

        def drawn(row):
            cells = [[noise_ref[WAYS * row + k, span, :] for span in spans] for k in range(WAYS)]
            if row not in own:
                scales = [spread(root_ref, k, row) for k in range(WAYS)]
                cells = [[cell * scales[k] for cell in cells[k]] for k in range(WAYS)]
            return cells

        def stepped(step, row):
            if (step, row - STEPS) in early_rows(tile_rows):
                first = WAYS * early_rows(tile_rows).index((step, row - STEPS))
                return [[early_ref[first + k, span, :] for span in spans] for k in range(WAYS)]
            past = known[step - 1]
            keep = [spread(keep_ref, k, row) for k in range(WAYS)]
            gain = [spread(gain_ref, k, row) for k in range(WAYS)]
            fresh = [
                step_on(*([cells[k][part] for k in range(WAYS)] for cells in (
                    past[row - 1], past[row], past[row + 1]
                )), keep, gain, run)
                for part in range(TOGETHER)
            ]
            return [[fresh[part][k] for part in range(TOGETHER)] for k in range(WAYS)]

        for top in range(rows):
            known[0][top] = drawn(top)
            for step in range(1, STEPS + 1):
                row = top - step
                if row < step:
                    break
                known[step][row] = stepped(step, row)
                del known[step - 1][row - 1]
        for row in range(out_rows):
            done = known[STEPS][row + STEPS]
            for k in range(parts):
                for part in range(TOGETHER):
                    one, two = done[2 * k][part], done[2 * k + 1][part]
                    low = jnp.where(lower, one, pltpu.roll(two, run, 1))
                    high = jnp.where(lower, pltpu.roll(one, run, 1), two)
                    state = jnp.concatenate([low, high], 0)
                    head = state.astype(BF16)
                    tail = (state - head.astype(F32)).astype(BF16)
                    first = row * columns + k * LANES
                    for place, piece in enumerate((head, tail, head)):
                        start = place * levels + (bundle * TOGETHER + part) * 2 * SUB
                        at = pl.ds(pl.multiple_of(start, 2 * SUB), 2 * SUB)
                        state_ref[at, first : first + LANES] = piece
        return carry

    lax.fori_loop(0, height // SUB // TOGETHER, diffuse, 0)

    bunch = 2 * SUB
    for row in range(out_rows):
        mixed = jnp.dot(
            factor_ref[...],
            state_ref[:, row * columns : (row + 1) * columns],
            preferred_element_type=F32,
        )
        scaled = (mixed * scales[row : row + 1]).astype(BF16)
        for part in range(levels // bunch):
            first = (part * out_rows + row) * bunch
            field_ref[first : first + bunch, :] = scaled[part * bunch : (part + 1) * bunch]

    col = column_of(iota((columns, 2 * LANES), 0), columns).astype(BF16)

    def positions(pair, first):
        tails = [recv_ref[2 * pair + k, parts * tile_rows :, :].astype(F32) for k in range(2)]
        tail = jnp.concatenate(tails, 1)
        return tail[first : first + 1], tail[first + 1 : first + 2] + tail[first + 2 : first + 3]

    def make_hat(pair, slot):
        near, frac_x = positions(pair, parts)
        hat_ref[slot] = jnp.where(
            col == near.astype(BF16),
            (1.0 - frac_x).astype(BF16),
            jnp.where(col == (near + 1.0).astype(BF16), frac_x.astype(BF16), jnp.zeros_like(col)),
        )

    def answer(pair, hat):
        along = jnp.dot(field_ref[...], hat, preferred_element_type=F32)
        pos_y = sum(positions(pair, parts + 3))
        weights = [jnp.maximum(1.0 - jnp.abs(pos_y - float(row)), 0.0) for row in range(out_rows)]
        for part in range(levels // bunch):
            terms = []
            for row in range(out_rows):
                first = (part * out_rows + row) * bunch
                terms.append(along[first : first + bunch] * weights[row])
            while len(terms) > 1:
                paired = [one + two for one, two in zip(terms[::2], terms[1::2])]
                terms = paired + terms[2 * len(paired) :]
            total = terms[0]
            kept = min(bunch // QUAD, -(-(depth - part * bunch) // QUAD))
            at = slice(part * bunch // QUAD, part * bunch // QUAD + kept)
            rounded = total.astype(BF16)[: kept * QUAD]
            for half in range(2):
                lanes = slice(half * LANES, (half + 1) * LANES)
                prof_ref[2 * pair + half, at] = rounded[:, lanes].reshape(kept, QUAD, LANES)

    def some_pairs(step, carry):
        for slot in range(PAIRS):
            make_hat(step * PAIRS + slot, slot)
        for slot in range(PAIRS):
            answer(step * PAIRS + slot, hat_ref[slot])
            if (slot + 1) % SENT == 0:
                sending((step * PAIRS + slot + 1) // SENT - 1).start()
        return carry

    def sending(batch):
        at = pl.ds(batch * 2 * SENT, 2 * SENT)
        return pltpu.make_async_copy(prof_ref.at[at], prof_hbm.at[at], sems.at[batch])

    lax.fori_loop(0, tiles // (2 * PAIRS), some_pairs, 0)
    for batch in range(tiles // (2 * SENT)):
        sending(batch).wait()


def weave_kernel(field_ref, out_ref, swap_ref, flat_ref):
    size = swap_ref.shape[0]
    bunch = 2 * SUB
    into, source = iota((size, size), 0), iota((size, size), 1)
    high, low = lax.shift_right_logical(into, 4), into & (bunch - 1)
    swap_ref[...] = (source == low * bunch + high).astype(BF16)
    depth, tile_rows, columns = out_ref.shape
    levels = field_ref.shape[0] // (tile_rows + 1)
    square = (columns, columns)
    weave = (iota(square, 1) == column_of(iota(square, 0), columns)).astype(BF16)
    woven = jnp.dot(field_ref[...], weave, preferred_element_type=F32)
    bunch = 2 * SUB
    for part in range(levels // bunch):
        for row in range(tile_rows):
            first = (part * (tile_rows + 1) + row) * bunch
            flat_ref[part * bunch : (part + 1) * bunch, row, :] = woven[first : first + bunch]
    out_ref[...] = flat_ref[:depth].astype(BF16)


def unpack_kernel(order, given_ref, swap_ref, out_ref, ready_ref, sems):
    depth, owners, _ = out_ref.shape
    bunch = 2 * SUB
    copies = []
    held = QUAD * given_ref.shape[1]
    for part, start in enumerate(range(0, depth, bunch)):
        end = min(start + bunch, depth)
        taken = min(start, held - bunch)
        for first in range(0, owners, bunch):
            rows = jnp.concatenate(
                [
                    given_ref[order.index(owner), taken // QUAD : (taken + bunch) // QUAD].reshape(
                        bunch, LANES
                    )
                    for owner in range(first, first + bunch)
                ],
                0,
            )
            turned = jnp.dot(swap_ref[...], rows, preferred_element_type=F32).astype(BF16)
            turned = turned.reshape(bunch, bunch, LANES)[start - taken : end - taken]
            ready_ref[start:end, first : first + bunch, :] = turned
        copies.append(
            pltpu.make_async_copy(ready_ref.at[start:end], out_ref.at[start:end], sems.at[part])
        )
        copies[-1].start()
    for copy in copies:
        copy.wait()


def body(
    noise_seeds, diffusivity, wet_mask, vert_factor, norm_scale, obs_cell, obs_frac, obs_count
):
    tile_rows, columns = diffusivity.shape
    depth = vert_factor.shape[0]
    levels = up(depth, 2 * SUB)
    tiles = lax.axis_size("tile")
    total_rows = tile_rows * tiles
    groups = LANES * WAYS // columns
    rows = tile_rows + 1 + 2 * STEPS
    slots = obs_cell.shape[2]
    parts = columns // LANES
    square = jax.ShapeDtypeStruct((tile_rows, columns), F32)

    packed, kappa_split, norm_split = pl.pallas_call(
        pack_kernel,
        out_shape=(
            jax.ShapeDtypeStruct((tiles, parts * tile_rows + SUB, LANES), BF16),
            square,
            square,
        ),
        in_specs=[VMEM] * 5 + [SMEM],
        out_specs=(VMEM,) * 3,
        name="pack",
    )(diffusivity, wet_mask, norm_scale, obs_cell[0], obs_frac[0], obs_count)
    order = visiting_order(tiles)
    exchange = dict(
        axis_name="tile", split_axis=0, concat_axis=0, tiled=True, axis_index_groups=[order]
    )
    received = lax.all_to_all(packed, **exchange)

    own = pltpu.VMEM((WAYS, up(tile_rows, SUB) + SUB, LANES), F32)
    early = len(early_rows(tile_rows))
    noise, ahead, *settled = pl.pallas_call(
        lambda *refs: noise_kernel(total_rows, tile_rows, columns, *refs),
        out_shape=(
            pltpu.VMEM((WAYS * rows, levels // groups, LANES), F32),
            pltpu.VMEM((WAYS * early, levels // groups, LANES), F32),
            pltpu.VMEM(diffusivity.shape, F32),
            pltpu.VMEM(diffusivity.shape, F32),
            pltpu.VMEM((levels, 3 * levels), BF16),
        ),
        in_specs=[SMEM, VMEM, VMEM, VMEM],
        out_specs=(VMEM,) * 5,
        scratch_shapes=[own, own, own, pltpu.VMEM((levels, up(3 * levels, LANES)), F32)],
        name="noise",
        compiler_params=LIMIT,
    )(*(distant(part) for part in (noise_seeds, kappa_split, norm_split, vert_factor)))

    coefficients = pltpu.VMEM((WAYS, up(rows, SUB), LANES), F32)
    answers, field = pl.pallas_call(
        lambda *refs: field_kernel(tiles, *refs),
        out_shape=(
            pltpu.HBM((tiles, up(depth, QUAD) // QUAD, QUAD, slots), BF16),
            pltpu.VMEM(((tile_rows + 1) * levels, columns), BF16),
        ),
        in_specs=[VMEM] * 6,
        out_specs=(ANY, VMEM),
        scratch_shapes=[
            pltpu.VMEM((up(rows, SUB), columns), F32),
            coefficients,
            coefficients,
            coefficients,
            pltpu.VMEM((3 * levels, (tile_rows + 1) * columns), BF16),
            pltpu.VMEM((PAIRS, columns, 2 * LANES), BF16),
            pltpu.VMEM((tiles, up(depth, QUAD) // QUAD, QUAD, slots), BF16),
            pltpu.SemaphoreType.DMA((tiles // (2 * SENT),)),
        ],
        name="field",
        compiler_params=LIMIT,
    )(
        *(resident(part) for part in (noise, ahead, received, *settled))
    )
    gathered = lax.all_to_all(answers, **exchange)
    perturbation, swap = pl.pallas_call(
        weave_kernel,
        out_shape=(
            jax.ShapeDtypeStruct((depth, tile_rows, columns), BF16),
            pltpu.VMEM((4 * SUB * SUB, 4 * SUB * SUB), BF16),
        ),
        in_specs=[VMEM],
        out_specs=(VMEM, VMEM),
        scratch_shapes=[pltpu.VMEM((levels, tile_rows, columns), F32)],
        name="weave",
        compiler_params=LIMIT,
    )(resident(field))
    chunks = levels // (2 * SUB)
    profiles = pl.pallas_call(
        lambda *refs: unpack_kernel(order, *refs),
        out_shape=jax.ShapeDtypeStruct((depth, tiles, slots), BF16),
        in_specs=[VMEM, VMEM],
        out_specs=ANY,
        scratch_shapes=[
            pltpu.VMEM((levels, tiles, slots), BF16),
            pltpu.SemaphoreType.DMA((chunks,)),
        ],
        name="unpack",
        compiler_params=LIMIT,
    )(resident(gathered), resident(swap))
    return (perturbation, jnp.transpose(profiles, (1, 0, 2))[None])


def solution(mesh):
    in_specs = (
        P("member"),
        P("tile", None),
        P("tile", None),
        P(),
        P("tile", None),
        P("tile", None, None),
        P("tile", None, None, None),
        P("tile", None),
    )
    out_specs = (P("member", "tile", None), P("tile", None, "member", None))
    return jax.shard_map(body, mesh=mesh, in_specs=in_specs, out_specs=out_specs, check_vma=False)
```

```python
import jax
import jax.numpy as jnp
from jax import lax
from jax.experimental import pallas as pl
from jax.experimental.pallas import tpu as pltpu
from jax.sharding import PartitionSpec as P

STEPS = 8
LANES = 128
SUB = 8
EXACT = lax.Precision.HIGHEST
F32 = jnp.float32
BF16 = jnp.bfloat16
WAYS = 4
TOGETHER = 5
PAIRS = 8
SENT = 2
QUAD = 4
I32 = jnp.int32
GOLDEN = -1640531535
ROOT12 = 3.4641016151377544
VMEM = pl.BlockSpec(memory_space=pltpu.VMEM)
SMEM = pl.BlockSpec(memory_space=pltpu.SMEM)
ANY = pl.BlockSpec(memory_space=pl.ANY)
LIMIT = pltpu.CompilerParams(vmem_limit_bytes=24 << 20)


def resident(array):
    return pltpu.with_memory_space_constraint(array, pltpu.VMEM)


def distant(array):
    return pltpu.with_memory_space_constraint(array, pltpu.HBM)


def up(value, unit):
    return -(-value // unit) * unit


def wrapped(value):
    return (value + 2**31) % 2**32 - 2**31


def iota(shape, axis):
    return lax.broadcasted_iota(I32, shape, axis)


def visiting_order(tiles):
    pairs = tiles // 2
    ring = list(range(1, pairs, 2)) + list(range(0, pairs, 2))[::-1]
    turn = pairs // 4
    return [2 * pair + core for pair in ring[turn:] + ring[:turn] for core in (1, 0)]


def place_of(tile, tiles):
    order = visiting_order(tiles)
    return sum(jnp.where(tile == order[place], place, 0) for place in range(1, tiles))


def column_of(place, columns):
    run = columns // WAYS
    turn = sum(((place >= k * run).astype(I32) for k in range(1, WAYS)), jnp.zeros_like(place))
    return WAYS * (place - turn * run) + turn


def pack_kernel(
    diff_ref, wet_ref, norm_ref, cell_ref, frac_ref, count_ref, out_ref, kappa_out, norm_out
):
    tile_rows, columns = diff_ref.shape
    owners = cell_ref.shape[0]
    order = visiting_order(owners)
    kappa = diff_ref[...] * wet_ref[...].astype(F32)
    square = (columns, columns)
    parting = (iota(square, 0) == column_of(iota((1, columns), 1), columns)).astype(F32)
    both = jnp.concatenate([kappa, norm_ref[...]], 0)
    parted = jnp.dot(both, parting, precision=EXACT, preferred_element_type=F32)
    kappa_out[...] = parted[:tile_rows]
    norm_out[...] = parted[tile_rows:]
    parts = columns // LANES
    halo = jnp.concatenate(
        [parted[:tile_rows, k * LANES : (k + 1) * LANES] for k in range(parts)], 0
    ).astype(BF16)
    norms = [parted[tile_rows : tile_rows + 1, k * LANES : (k + 1) * LANES] for k in range(parts)]
    cell = cell_ref[...]
    row = jnp.zeros_like(cell)
    for step in range(1, tile_rows):
        row = row + (cell >= step * columns).astype(I32)
    col = (cell - row * columns).astype(F32)
    row = row.astype(F32)
    frac_y, frac_x = frac_ref[:, 0, :], frac_ref[:, 1, :]
    high_y, high_x = (frac.astype(BF16).astype(F32) for frac in (frac_y, frac_x))
    low_y, low_x = frac_y - high_y, frac_x - high_x
    lane = iota((1, LANES), 1)
    for owner in range(owners):
        at = slice(owner, owner + 1)
        live = lane < count_ref[:, owner : owner + 1]
        tail = jnp.concatenate(
            norms + [col[at], high_x[at], low_x[at]]
            + [jnp.where(live, row[at], -16.0), high_y[at], low_y[at]],
            0,
        )
        at = order.index(owner)
        out_ref[at, : parts * tile_rows, :] = halo
        out_ref[at, parts * tile_rows :, :] = tail.astype(BF16)


def mix(hashed):
    hashed = (hashed ^ lax.shift_right_logical(hashed, 16)) * -2048144789
    hashed = (hashed ^ lax.shift_right_logical(hashed, 13)) * -1028477387
    hashed = hashed ^ lax.shift_right_logical(hashed, 16)
    return hashed


def spread(ref, k, row):
    return ref[k, pl.ds(row, SUB, stride=0), :]


def couple(root, rows, root_ref, keep_ref, gain_ref):
    run = root.shape[1] // WAYS
    groups = LANES // run
    lane = iota((1, LANES), 1)
    roots = []
    for k in range(WAYS):
        vector = root[:, (k // groups) * LANES : (k // groups + 1) * LANES]
        turned = pltpu.roll(vector, run, 1)
        keeps = (lane >= run) if k % groups else (lane < run)
        roots.append(jnp.where(keeps, vector, turned))
        root_ref[k, : root.shape[0]] = roots[k]
    low, high = (lane == 0) | (lane == run), (lane == run - 1) | (lane == LANES - 1)
    inner = slice(1, rows - 1)
    west = [jnp.where(low, 0.0, pltpu.roll(roots[-1], 1, 1))] + roots[:-1]
    east = roots[1:] + [jnp.where(high, 0.0, pltpu.roll(roots[0], LANES - 1, 1))]
    for k in range(WAYS):
        near = root_ref[k, : rows - 2] + root_ref[k, 2:rows] + (west[k] + east[k])[inner]
        keep_ref[k, inner] = 1.0 - roots[k][inner] * near
        gain_ref[k, inner] = roots[k][inner] * roots[k][inner]


def step_on(above, here, under, keep, gain, run):
    lanes = iota((SUB, LANES), 1)
    low, high = (lanes == 0) | (lanes == run), (lanes == run - 1) | (lanes == LANES - 1)
    west = [jnp.where(low, 0.0, pltpu.roll(here[-1], 1, 1))] + here[:-1]
    east = here[1:] + [jnp.where(high, 0.0, pltpu.roll(here[0], LANES - 1, 1))]
    return [
        keep[k] * here[k] + gain[k] * ((above[k] + under[k]) + (west[k] + east[k]))
        for k in range(WAYS)
    ]


def early_rows(tile_rows):
    steps = range(1, min(STEPS, (tile_rows - 1) // 2) + 1)
    return [(step, row) for step in steps for row in range(step, tile_rows - step)]


def noise_kernel(
    total_rows, tile_rows, columns, seed_ref, kappa_ref, norm_ref, vert_ref,
    out_ref, early_ref, kappa_out, norm_out, factor_ref, root_ref, keep_ref, gain_ref, vert_pad,
):
    kappa_out[...] = kappa_ref[...]
    norm_out[...] = norm_ref[...]
    depth, levels = vert_ref.shape[0], factor_ref.shape[0]
    vert_pad[...] = jnp.zeros_like(vert_pad)
    vert_pad[:depth, :depth] = vert_ref[...]
    vert = vert_pad[...]
    head = vert.astype(BF16).astype(F32)
    factor = head + pltpu.roll(head, levels, 1) + pltpu.roll(vert - head, 2 * levels, 1)
    factor_ref[...] = factor.astype(BF16)[:, : 3 * levels]
    planes, height, _ = out_ref.shape
    couple(jnp.sqrt(kappa_ref[...]), tile_rows, root_ref, keep_ref, gain_ref)
    run = columns // WAYS
    groups = LANES // run
    first_row = lax.axis_index("tile") * tile_rows - STEPS
    step_level = wrapped(total_rows * columns * GOLDEN)
    shape = (SUB, LANES)
    group = sum(((iota(shape, 1) >= g * run).astype(I32) for g in range(1, groups)), 0)
    base = (iota(shape, 0) + SUB * group) * step_level
    base = base + (iota(shape, 1) - group * run) * wrapped(WAYS * GOLDEN)
    gain = ROOT12 / 16777216.0
    shift = (0.5 / 16777216.0 - 0.5) * ROOT12
    origin = first_row * wrapped(columns * GOLDEN) + seed_ref[0]
    second = seed_ref[1]

    def one_tile(part, carry):
        start = origin + part * wrapped(groups * SUB * step_level)
        span = pl.ds(pl.multiple_of(part * SUB, SUB), SUB)
        known = {}
        for plane in range(planes):
            offset = start + wrapped(((plane // WAYS) * columns + plane % WAYS) * GOLDEN)
            hashed = mix(mix(base + offset) ^ second)
            drawn = lax.shift_right_logical(hashed, 8).astype(F32)
            drawn = drawn * gain + shift
            row = plane // WAYS - STEPS
            if 0 <= row < tile_rows:
                drawn = drawn * spread(root_ref, plane % WAYS, row)
                known.setdefault((0, row), []).append(drawn)
            out_ref[plane, span, :] = drawn
        for place, (step, row) in enumerate(early_rows(tile_rows)):
            known[step, row] = step_on(
                known[step - 1, row - 1], known[step - 1, row], known[step - 1, row + 1],
                [spread(keep_ref, k, row) for k in range(WAYS)],
                [spread(gain_ref, k, row) for k in range(WAYS)],
                run,
            )
            for k in range(WAYS):
                early_ref[WAYS * place + k, span, :] = known[step, row][k]
        return carry

    lax.fori_loop(0, height // SUB, one_tile, 0)


def field_kernel(
    tiles, noise_ref, early_ref, recv_ref, kappa_ref, norm_ref, factor_ref, prof_hbm, field_ref,
    halo_ref, root_ref, keep_ref, gain_ref, state_ref, hat_ref, prof_ref, sems,
):
    planes, height, _ = noise_ref.shape
    rows = planes // WAYS
    tile_rows, columns = norm_ref.shape
    run = columns // WAYS
    groups = LANES // run
    levels = height * groups
    depth = QUAD * prof_ref.shape[1]
    out_rows = tile_rows + 1
    parts = columns // LANES
    tile = lax.axis_index("tile")

    halo_ref[...] = jnp.zeros_like(halo_ref)
    halo_ref[tile_rows : 2 * tile_rows] = kappa_ref[...]
    for place, shift, count in ((0, -1, tile_rows), (2, 1, tile_rows), (3, 2, 1)):
        source = tile + shift
        valid = ((source >= 0) & (source < tiles)).astype(F32)
        given = recv_ref[place_of(jnp.clip(source, 0, tiles - 1), tiles), : parts * tile_rows, :].astype(F32) * valid
        for k in range(parts):
            halo_ref[place * tile_rows : place * tile_rows + count, k * LANES : (k + 1) * LANES] = (
                given[k * tile_rows : k * tile_rows + count]
            )
    root = jnp.sqrt(halo_ref[...])
    couple(root, rows, root_ref, keep_ref, gain_ref)
    kappa = halo_ref[STEPS : STEPS + out_rows]
    wet = kappa > 0.0
    inverse = jnp.where(wet, root[STEPS : STEPS + out_rows] / jnp.where(wet, kappa, 1.0), 0.0)
    below = recv_ref[place_of(jnp.clip(tile + 1, 0, tiles - 1), tiles), parts * tile_rows :, :].astype(F32)
    norm_below = jnp.concatenate([below[k : k + 1] for k in range(parts)], 1)
    scales = inverse * jnp.concatenate([norm_ref[...], norm_below], 0)

    lower = iota((SUB, LANES), 1) < run

    def diffuse(bundle, carry):
        spans = [
            pl.ds(pl.multiple_of((bundle * TOGETHER + part) * SUB, SUB), SUB) for part in range(TOGETHER)
        ]
        known = [{} for _ in range(STEPS + 1)]

        own = range(STEPS, STEPS + tile_rows)

        def drawn(row):
            cells = [[noise_ref[WAYS * row + k, span, :] for span in spans] for k in range(WAYS)]
            if row not in own:
                scales = [spread(root_ref, k, row) for k in range(WAYS)]
                cells = [[cell * scales[k] for cell in cells[k]] for k in range(WAYS)]
            return cells

        def stepped(step, row):
            if (step, row - STEPS) in early_rows(tile_rows):
                first = WAYS * early_rows(tile_rows).index((step, row - STEPS))
                return [[early_ref[first + k, span, :] for span in spans] for k in range(WAYS)]
            past = known[step - 1]
            keep = [spread(keep_ref, k, row) for k in range(WAYS)]
            gain = [spread(gain_ref, k, row) for k in range(WAYS)]
            fresh = [
                step_on(*([cells[k][part] for k in range(WAYS)] for cells in (
                    past[row - 1], past[row], past[row + 1]
                )), keep, gain, run)
                for part in range(TOGETHER)
            ]
            return [[fresh[part][k] for part in range(TOGETHER)] for k in range(WAYS)]

        for top in range(rows):
            known[0][top] = drawn(top)
            for step in range(1, STEPS + 1):
                row = top - step
                if row < step:
                    break
                known[step][row] = stepped(step, row)
                del known[step - 1][row - 1]
        for row in range(out_rows):
            done = known[STEPS][row + STEPS]
            for k in range(parts):
                for part in range(TOGETHER):
                    one, two = done[2 * k][part], done[2 * k + 1][part]
                    low = jnp.where(lower, one, pltpu.roll(two, run, 1))
                    high = jnp.where(lower, pltpu.roll(one, run, 1), two)
                    state = jnp.concatenate([low, high], 0)
                    head = state.astype(BF16)
                    tail = (state - head.astype(F32)).astype(BF16)
                    first = row * columns + k * LANES
                    for place, piece in enumerate((head, tail, head)):
                        start = place * levels + (bundle * TOGETHER + part) * 2 * SUB
                        at = pl.ds(pl.multiple_of(start, 2 * SUB), 2 * SUB)
                        state_ref[at, first : first + LANES] = piece
        return carry

    lax.fori_loop(0, height // SUB // TOGETHER, diffuse, 0)

    bunch = 2 * SUB
    for row in range(out_rows):
        mixed = jnp.dot(
            factor_ref[...],
            state_ref[:, row * columns : (row + 1) * columns],
            preferred_element_type=F32,
        )
        scaled = (mixed * scales[row : row + 1]).astype(BF16)
        for part in range(levels // bunch):
            first = (part * out_rows + row) * bunch
            field_ref[first : first + bunch, :] = scaled[part * bunch : (part + 1) * bunch]

    col = column_of(iota((columns, 2 * LANES), 0), columns).astype(BF16)

    def positions(pair, first):
        tails = [recv_ref[2 * pair + k, parts * tile_rows :, :].astype(F32) for k in range(2)]
        tail = jnp.concatenate(tails, 1)
        return tail[first : first + 1], tail[first + 1 : first + 2] + tail[first + 2 : first + 3]

    def make_hat(pair, slot):
        near, frac_x = positions(pair, parts)
        hat_ref[slot] = jnp.where(
            col == near.astype(BF16),
            (1.0 - frac_x).astype(BF16),
            jnp.where(col == (near + 1.0).astype(BF16), frac_x.astype(BF16), jnp.zeros_like(col)),
        )

    def answer(pair, hat):
        along = jnp.dot(field_ref[...], hat, preferred_element_type=F32)
        pos_y = sum(positions(pair, parts + 3))
        weights = [jnp.maximum(1.0 - jnp.abs(pos_y - float(row)), 0.0) for row in range(out_rows)]
        for part in range(levels // bunch):
            terms = []
            for row in range(out_rows):
                first = (part * out_rows + row) * bunch
                terms.append(along[first : first + bunch] * weights[row])
            while len(terms) > 1:
                paired = [one + two for one, two in zip(terms[::2], terms[1::2])]
                terms = paired + terms[2 * len(paired) :]
            total = terms[0]
            kept = min(bunch // QUAD, -(-(depth - part * bunch) // QUAD))
            at = slice(part * bunch // QUAD, part * bunch // QUAD + kept)
            rounded = total.astype(BF16)[: kept * QUAD]
            for half in range(2):
                lanes = slice(half * LANES, (half + 1) * LANES)
                prof_ref[2 * pair + half, at] = rounded[:, lanes].reshape(kept, QUAD, LANES)

    def some_pairs(step, carry):
        for slot in range(PAIRS):
            make_hat(step * PAIRS + slot, slot)
        for slot in range(PAIRS):
            answer(step * PAIRS + slot, hat_ref[slot])
            if (slot + 1) % SENT == 0:
                sending((step * PAIRS + slot + 1) // SENT - 1).start()
        return carry

    def sending(batch):
        at = pl.ds(batch * 2 * SENT, 2 * SENT)
        return pltpu.make_async_copy(prof_ref.at[at], prof_hbm.at[at], sems.at[batch])

    lax.fori_loop(0, tiles // (2 * PAIRS), some_pairs, 0)
    for batch in range(tiles // (2 * SENT)):
        sending(batch).wait()


def weave_kernel(field_ref, out_ref, swap_ref, flat_ref):
    size = swap_ref.shape[0]
    bunch = 2 * SUB
    into, source = iota((size, size), 0), iota((size, size), 1)
    high, low = lax.shift_right_logical(into, 4), into & (bunch - 1)
    swap_ref[...] = (source == low * bunch + high).astype(BF16)
    depth, tile_rows, columns = out_ref.shape
    levels = field_ref.shape[0] // (tile_rows + 1)
    square = (columns, columns)
    weave = (iota(square, 1) == column_of(iota(square, 0), columns)).astype(BF16)
    woven = jnp.dot(field_ref[...], weave, preferred_element_type=F32)
    bunch = 2 * SUB
    for part in range(levels // bunch):
        for row in range(tile_rows):
            first = (part * (tile_rows + 1) + row) * bunch
            flat_ref[part * bunch : (part + 1) * bunch, row, :] = woven[first : first + bunch]
    out_ref[...] = flat_ref[:depth].astype(BF16)


def unpack_kernel(order, given_ref, swap_ref, out_ref, ready_ref, sems):
    depth, owners, _ = out_ref.shape
    bunch = 2 * SUB
    copies = []
    held = QUAD * given_ref.shape[1]
    for part, start in enumerate(range(0, depth, bunch)):
        end = min(start + bunch, depth)
        taken = min(start, held - bunch)
        for first in range(0, owners, bunch):
            rows = jnp.concatenate(
                [
                    given_ref[order.index(owner), taken // QUAD : (taken + bunch) // QUAD].reshape(
                        bunch, LANES
                    )
                    for owner in range(first, first + bunch)
                ],
                0,
            )
            turned = jnp.dot(swap_ref[...], rows, preferred_element_type=F32).astype(BF16)
            turned = turned.reshape(bunch, bunch, LANES)[start - taken : end - taken]
            ready_ref[start:end, first : first + bunch, :] = turned
        copies.append(
            pltpu.make_async_copy(ready_ref.at[start:end], out_ref.at[start:end], sems.at[part])
        )
        copies[-1].start()
    for copy in copies:
        copy.wait()


def body(
    noise_seeds, diffusivity, wet_mask, vert_factor, norm_scale, obs_cell, obs_frac, obs_count
):
    tile_rows, columns = diffusivity.shape
    depth = vert_factor.shape[0]
    levels = up(depth, 2 * SUB)
    tiles = lax.axis_size("tile")
    total_rows = tile_rows * tiles
    groups = LANES * WAYS // columns
    rows = tile_rows + 1 + 2 * STEPS
    slots = obs_cell.shape[2]
    parts = columns // LANES
    square = jax.ShapeDtypeStruct((tile_rows, columns), F32)

    packed, kappa_split, norm_split = pl.pallas_call(
        pack_kernel,
        out_shape=(
            jax.ShapeDtypeStruct((tiles, parts * tile_rows + SUB, LANES), BF16),
            square,
            square,
        ),
        in_specs=[VMEM] * 6,
        out_specs=(VMEM,) * 3,
        name="pack",
    )(diffusivity, wet_mask, norm_scale, obs_cell[0], obs_frac[0], obs_count)
    order = visiting_order(tiles)
    exchange = dict(
        axis_name="tile", split_axis=0, concat_axis=0, tiled=True, axis_index_groups=[order]
    )
    received = lax.all_to_all(packed, **exchange)

    own = pltpu.VMEM((WAYS, up(tile_rows, SUB) + SUB, LANES), F32)
    early = len(early_rows(tile_rows))
    noise, ahead, *settled = pl.pallas_call(
        lambda *refs: noise_kernel(total_rows, tile_rows, columns, *refs),
        out_shape=(
            pltpu.VMEM((WAYS * rows, levels // groups, LANES), F32),
            pltpu.VMEM((WAYS * early, levels // groups, LANES), F32),
            pltpu.VMEM(diffusivity.shape, F32),
            pltpu.VMEM(diffusivity.shape, F32),
            pltpu.VMEM((levels, 3 * levels), BF16),
        ),
        in_specs=[SMEM, VMEM, VMEM, VMEM],
        out_specs=(VMEM,) * 5,
        scratch_shapes=[own, own, own, pltpu.VMEM((levels, up(3 * levels, LANES)), F32)],
        name="noise",
        compiler_params=LIMIT,
    )(*(distant(part) for part in (noise_seeds, kappa_split, norm_split, vert_factor)))

    coefficients = pltpu.VMEM((WAYS, up(rows, SUB), LANES), F32)
    answers, field = pl.pallas_call(
        lambda *refs: field_kernel(tiles, *refs),
        out_shape=(
            pltpu.HBM((tiles, up(depth, QUAD) // QUAD, QUAD, slots), BF16),
            pltpu.VMEM(((tile_rows + 1) * levels, columns), BF16),
        ),
        in_specs=[VMEM] * 6,
        out_specs=(ANY, VMEM),
        scratch_shapes=[
            pltpu.VMEM((up(rows, SUB), columns), F32),
            coefficients,
            coefficients,
            coefficients,
            pltpu.VMEM((3 * levels, (tile_rows + 1) * columns), BF16),
            pltpu.VMEM((PAIRS, columns, 2 * LANES), BF16),
            pltpu.VMEM((tiles, up(depth, QUAD) // QUAD, QUAD, slots), BF16),
            pltpu.SemaphoreType.DMA((tiles // (2 * SENT),)),
        ],
        name="field",
        compiler_params=LIMIT,
    )(
        *(resident(part) for part in (noise, ahead, received, *settled))
    )
    gathered = lax.all_to_all(answers, **exchange)
    perturbation, swap = pl.pallas_call(
        weave_kernel,
        out_shape=(
            jax.ShapeDtypeStruct((depth, tile_rows, columns), BF16),
            pltpu.VMEM((4 * SUB * SUB, 4 * SUB * SUB), BF16),
        ),
        in_specs=[VMEM],
        out_specs=(VMEM, VMEM),
        scratch_shapes=[pltpu.VMEM((levels, tile_rows, columns), F32)],
        name="weave",
        compiler_params=LIMIT,
    )(resident(field))
    chunks = levels // (2 * SUB)
    profiles = pl.pallas_call(
        lambda *refs: unpack_kernel(order, *refs),
        out_shape=jax.ShapeDtypeStruct((depth, tiles, slots), BF16),
        in_specs=[VMEM, VMEM],
        out_specs=ANY,
        scratch_shapes=[
            pltpu.VMEM((levels, tiles, slots), BF16),
            pltpu.SemaphoreType.DMA((chunks,)),
        ],
        name="unpack",
        compiler_params=LIMIT,
    )(resident(gathered), resident(swap))
    return (perturbation, jnp.transpose(profiles, (1, 0, 2))[None])


def solution(mesh):
    in_specs = (
        P("member"),
        P("tile", None),
        P("tile", None),
        P(),
        P("tile", None),
        P("tile", None, None),
        P("tile", None, None, None),
        P("tile", None),
    )
    out_specs = (P("member", "tile", None), P("tile", None, "member", None))
    return jax.shard_map(body, mesh=mesh, in_specs=in_specs, out_specs=out_specs, check_vma=False)
```
